512 devices in a mesh: dp: 16 (over z, x_lo), space: 32 (over y, x_hi, core).
Axes of the slice: x: 4 (x_hi: 2, x_lo: 2; x = x_hi * 2 + x_lo), y: 8, z: 8, core: 2. Of those that a mesh axis runs over, the one named last changes fastest.
Arguments:
- features: bfloat16 [16, 64, 72, 2048], P('dp', 'space'), may hold values from -150 to 150
- depthwise: bfloat16 [2, 9, 2048], replicated, may hold values from -2 to 2
- pointwise: bfloat16 [2048, 512], replicated, may hold values from -0.125 to 0.125
- bn_gain: float32 [2, 2048], replicated, may hold values from 0.1 to 1.9
- cotangent: bfloat16 [16, 64, 72, 256], P('dp', 'space'), may hold values from -6 to 6
Outputs:
- block_out: bfloat16 [16, 64, 72, 256], P('dp', 'space')
- grad_pointwise: float32 [2048, 512], P('space')
- grad_depthwise: float32 [2, 9, 2048], P(None, None, 'space')
The draws below stay inside these ranges and needn't reach their ends.
All inputs are finite; a program needn't handle non-finite values.
Results may differ from the reference program's by a relative error of at most 0.001.
The reference program's roundings to bfloat16 on the way count: a program that leaves them out, or rounds other values in their place, can miss the bound.
Values may be sent and summed in bfloat16 or wider, within the bound.
No kernel may reach another device: no remote copies, remote signals or barrier semaphores. Data moves between devices by JAX's collectives and lax.ppermute only.
A program may use at most 64 MiB of HBM per device.

```python
import math
import jax
import jax.numpy as jnp
from jax import lax

C = 2048
O = 256
WIDTH = 72
NEAR_DILATION = 12
FAR_DILATION = 24
SAMPLES = 16
HEIGHT = 64


def draw_features(key, part):
    first_key, second_key = jax.random.split(key)
    full_shape = (SAMPLES, HEIGHT, WIDTH, C)
    values_base = jnp.clip(jax.random.normal(first_key, full_shape, jnp.float32), -5.0, 5.0)
    spread = math.log(10.0)
    channel_scale = jnp.exp(jax.random.uniform(second_key, (C,), jnp.float32, 0.0, spread))
    row_scale = jnp.exp(jnp.arange(HEIGHT, dtype=jnp.float32) * (math.log(3.0) / max(HEIGHT - 1, 1)))
    return (values_base * channel_scale * row_scale[None, :, None, None]).astype(jnp.bfloat16)


def steps_of(stream_key, dims, cuts, smallest, top_value):
    loudness = 1.0
    for dim, blocks in cuts:
        heights = jax.random.uniform(jax.random.fold_in(jax.random.fold_in(stream_key, 6), dim), (blocks,), jnp.float32, smallest / len(cuts), top_value / len(cuts))
        loudness = loudness * jnp.repeat(jnp.exp(heights), dims[dim] // blocks).reshape((-1,) + (1,) * (len(dims) - 1 - dim))
    return loudness


def gaussian(key, shape, width, reach, pieces=(), kind=jnp.bfloat16):
    level = steps_of(key, shape, pieces, -0.22, 0.18) if pieces else 1.0
    array = jax.random.normal(key, shape, jnp.float32) * width * level
    return jnp.minimum(jnp.maximum(array, -reach), reach).astype(kind)


def setup_inputs(seed: int = 0) -> dict:
    keys = jax.random.split(jax.random.key(seed), 6)
    features = draw_features(jax.random.fold_in(keys[5], 71), 0)
    depthwise = gaussian(keys[1], (2, 9, C), 9 ** -0.5, 2.0)
    pointwise = gaussian(keys[2], (C, 2 * O), C ** -0.5, 0.125)
    bn_gain = jnp.clip(1.0 + 0.18 * jax.random.normal(keys[3], (2, C), jnp.float32), 0.1, 1.9)
    cotangent = gaussian(keys[4], (SAMPLES, HEIGHT, WIDTH, O), 1.0, 6.0, ((0, 16), (1, 32)))
    return dict(features=features, depthwise=depthwise, pointwise=pointwise, bn_gain=bn_gain, cotangent=cotangent)


eps_norm = 1e-05

def shift_dim(input_values, offset, reduce_axis):
    if offset == 0:
        return input_values
    extent = abs(offset)
    length_here = input_values.shape[reduce_axis]
    padding = [(0, 0)] * input_values.ndim
    padding[reduce_axis] = (extent, extent)
    padded = jnp.pad(input_values, padding)
    return lax.slice_in_dim(padded, extent + offset, extent + offset + length_here, axis=reduce_axis)

def depthwise_out(sources, weights, dilation, col_axis):
    running_total = jnp.zeros(sources[1].shape, jnp.float32)
    for row_tap in range(3):
        for col_tap in range(3):
            moved = shift_dim(sources[row_tap], (col_tap - 1) * dilation, col_axis)
            running_total = running_total + weights[3 * row_tap + col_tap].astype(jnp.float32) * moved.astype(jnp.float32)
    return running_total

def depthwise_grad(sources, gradient_map, dilation, col_axis, sum_axes):
    results = []
    for row_tap in range(3):
        for col_tap in range(3):
            moved = shift_dim(sources[row_tap], (col_tap - 1) * dilation, col_axis)
            results.append(lax.optimization_barrier(jnp.sum(gradient_map.astype(jnp.float32) * moved.astype(jnp.float32), axis=sum_axes)))
    return jnp.stack(results)

def sample_sources(sample_snapshot, dilation):
    return (shift_dim(sample_snapshot, -dilation, 0), sample_snapshot, shift_dim(sample_snapshot, dilation, 0))

def reference(features, depthwise, pointwise, bn_gain, cotangent):
    dilation_rates = (NEAR_DILATION, FAR_DILATION)
    pixels = HEIGHT * WIDTH
    count = float(SAMPLES * HEIGHT * WIDTH)

    def branch_values(sample_snapshot):
        return jnp.stack([depthwise_out(sample_sources(sample_snapshot, dilation_rates[k]), depthwise[k], dilation_rates[k], 1) for k in range(2)]).astype(jnp.bfloat16)

    def first_pass(running_total, sample_snapshot):
        input_values = branch_values(sample_snapshot).astype(jnp.float32)
        return ((running_total[0] + lax.optimization_barrier(jnp.sum(input_values, axis=(1, 2))), running_total[1] + lax.optimization_barrier(jnp.sum(input_values * input_values, axis=(1, 2)))), None)
    zeros_pair = jnp.zeros((2, C), jnp.float32)
    (sum_vals, sum_squares), _ = lax.scan(first_pass, (zeros_pair, zeros_pair), features)
    batch_average = sum_vals / count
    variance = sum_squares / count - batch_average * batch_average
    inverse_deviation = lax.rsqrt(variance + eps_norm)[:, None, None, :]
    centred_values = batch_average[:, None, None, :]
    norm_gains = bn_gain[:, None, None, :]

    def local_pieces(sample_snapshot, gradient_map):
        input_values = branch_values(sample_snapshot).astype(jnp.float32)
        normalized_input = (input_values - centred_values) * inverse_deviation
        scaled_values = norm_gains * normalized_input
        used = jnp.maximum(scaled_values, 0.0).astype(jnp.bfloat16)
        flattened_used = used.reshape(2, pixels, C)
        gradient_rows = gradient_map.reshape(pixels, O)
        grad_used = jnp.stack([jnp.dot(gradient_rows, pointwise[:, k * O:(k + 1) * O].T, preferred_element_type=jnp.float32) for k in range(2)]).reshape(2, HEIGHT, WIDTH, C)
        normalized_gradient = jnp.where(scaled_values > 0, grad_used, 0.0) * norm_gains
        return (normalized_input, flattened_used, gradient_rows, normalized_gradient)

    def second_pass(running_total, inputs):
        sample_snapshot, gradient_map = inputs
        normalized_input, flattened_used, gradient_rows, normalized_gradient = local_pieces(sample_snapshot, gradient_map)
        branch_output = jnp.dot(flattened_used[0], pointwise[:, :O], preferred_element_type=jnp.float32) + jnp.dot(flattened_used[1], pointwise[:, O:], preferred_element_type=jnp.float32)
        branch_output = branch_output.astype(jnp.bfloat16).reshape(HEIGHT, WIDTH, O)
        weight_products = jnp.concatenate([jnp.dot(flattened_used[k].T, gradient_rows, preferred_element_type=jnp.float32) for k in range(2)], axis=1)
        return ((running_total[0] + weight_products, running_total[1] + lax.optimization_barrier(jnp.sum(normalized_gradient, axis=(1, 2))), running_total[2] + lax.optimization_barrier(jnp.sum(normalized_gradient * normalized_input, axis=(1, 2)))), branch_output)
    (grad_pw, first_sums, second_sums), outputs = lax.scan(second_pass, (jnp.zeros((C, 2 * O), jnp.float32), zeros_pair, zeros_pair), (features, cotangent))
    mean_first_moment = (first_sums / count)[:, None, None, :]
    mean_second_moment = (second_sums / count)[:, None, None, :]

    def third_pass(running_total, inputs):
        sample_snapshot, gradient_map = inputs
        normalized_input, flattened_used, gradient_rows, normalized_gradient = local_pieces(sample_snapshot, gradient_map)
        gradient_values = (inverse_deviation * (normalized_gradient - mean_first_moment - normalized_input * mean_second_moment)).astype(jnp.bfloat16)
        grads = jnp.stack([depthwise_grad(sample_sources(sample_snapshot, dilation_rates[k]), gradient_values[k], dilation_rates[k], 1, (0, 1)) for k in range(2)])
        return (running_total + grads, None)
    grad_dw, _ = lax.scan(third_pass, jnp.zeros((2, 9, C), jnp.float32), (features, cotangent))
    return (outputs, grad_pw, grad_dw)
```

```python
import jax
import jax.numpy as jnp
from jax import lax
from jax.sharding import Mesh, PartitionSpec as P

NEAR_DILATION = 12
FAR_DILATION = 24
DILATIONS = (NEAR_DILATION, FAR_DILATION)
eps_norm = 1e-05

GROUP = ("y", "xh")
ROWS = ("dp", "core")
f32 = jnp.float32
bf16 = jnp.bfloat16


def exchange(value, axes):
    return lax.all_to_all(value, axes, 0, 0, tiled=True)


def shift_dim(values, offset, axis):
    if offset == 0:
        return values
    extent = abs(offset)
    length = values.shape[axis]
    padding = [(0, 0)] * values.ndim
    padding[axis] = (extent, extent)
    return lax.slice_in_dim(jnp.pad(values, padding), extent + offset, extent + offset + length, axis=axis)


def tap(values, row_steps, col_steps):
    return shift_dim(shift_dim(values, row_steps, 0), col_steps, 2)


def body(features, depthwise, pointwise, bn_gain, cotangent):
    _, row_count, width, channels = features.shape
    outs = cotangent.shape[3]
    groups = lax.axis_size(GROUP)
    peers = lax.axis_size(ROWS)
    samples = lax.axis_size("dp")
    cores = lax.axis_size("core")
    block = channels // groups
    share = block // cores
    pixels = row_count * width
    row_step = row_count * cores
    count = float(samples * groups * cores * pixels)
    mine = lax.axis_index(GROUP)
    core = lax.axis_index("core")

    sent = features.reshape(pixels, groups, block).transpose(1, 0, 2)
    held = exchange(sent, GROUP).reshape(groups, row_count, width, block)
    cot = exchange(jnp.broadcast_to(cotangent.reshape(1, pixels, outs), (groups, pixels, outs)), GROUP)
    cot = cot.reshape(groups * pixels, outs)
    taps = lax.dynamic_slice_in_dim(depthwise, mine * block, block, 2).astype(f32)
    gain = lax.dynamic_slice_in_dim(bn_gain, mine * block, block, 1)
    maps = lax.dynamic_slice_in_dim(pointwise, mine * block, block, 0)

    z = []
    sums = []
    for k, dilation in enumerate(DILATIONS):
        total = jnp.zeros(held.shape, f32)
        for a in range(3):
            for b in range(3):
                moved = tap(held, (a - 1) * dilation // row_step, (b - 1) * dilation)
                total = total + taps[k, 3 * a + b] * moved.astype(f32)
        value = total.astype(bf16)
        z.append(value)
        value = value.astype(f32)
        sums += [jnp.sum(value, axis=(0, 1, 2)), jnp.sum(value * value, axis=(0, 1, 2))]
    sums = jnp.pad(jnp.stack(sums), ((0, 4), (0, 0)))
    sums = jnp.sum(exchange(jnp.broadcast_to(sums, (peers, 8, block)), ROWS), axis=0)

    inv, xhat, used, dxhat, seconds, grads = [], [], [], [], [], []
    for k in range(2):
        average = sums[2 * k] / count
        variance = sums[2 * k + 1] / count - average * average
        inv.append(lax.rsqrt(variance + eps_norm))
        xhat.append((z[k].astype(f32) - average) * inv[k])
        scaled = gain[k] * xhat[k]
        used.append(jnp.maximum(scaled, 0.0).astype(bf16).reshape(groups * pixels, block))
        back = lax.dot_general(
            cot, maps[:, k * outs : (k + 1) * outs], (((1,), (1,)), ((), ())), preferred_element_type=f32
        ).reshape(scaled.shape)
        dxhat.append(jnp.where(scaled > 0, back, 0.0) * gain[k])
        seconds += [jnp.sum(dxhat[k], axis=(0, 1, 2)), jnp.sum(dxhat[k] * xhat[k], axis=(0, 1, 2))]
        grads.append(lax.dot_general(used[k], cot, (((0,), (0,)), ((), ())), preferred_element_type=f32))

    sent = jnp.concatenate([u.reshape(groups, pixels, block) for u in used], axis=2)
    whole = exchange(sent, GROUP)
    kernel = pointwise.reshape(groups, block, 2, outs).transpose(0, 2, 1, 3).reshape(groups * 2 * block, outs)
    block_out = jnp.dot(
        whole.transpose(1, 0, 2).reshape(pixels, groups * 2 * block), kernel, preferred_element_type=f32
    )
    block_out = block_out.astype(bf16).reshape(1, row_count, width, outs)

    part = share // samples
    grads = jnp.concatenate(grads, axis=1).reshape(cores, samples, part * 2 * outs)
    grads = grads.transpose(1, 0, 2).reshape(peers, part * 2 * outs // block, block)
    seconds = jnp.broadcast_to(jnp.pad(jnp.stack(seconds), ((0, 4), (0, 0))), (peers, 8, block))
    got = jnp.sum(exchange(jnp.concatenate([grads, seconds], axis=1), ROWS), axis=0)
    lines = grads.shape[1]
    piece, seconds = got[:lines], got[lines:]

    grad_dw = []
    for k, dilation in enumerate(DILATIONS):
        dz = (inv[k] * (dxhat[k] - seconds[2 * k] / count - xhat[k] * (seconds[2 * k + 1] / count))).astype(bf16)
        dz = dz.astype(f32)
        for a in range(3):
            for b in range(3):
                moved = tap(held, (a - 1) * dilation // row_step, (b - 1) * dilation)
                grad_dw.append(jnp.sum(dz * moved.astype(f32), axis=(0, 1, 2)))
    grad_dw = jnp.stack(grad_dw).reshape(2, 9, cores, share).transpose(2, 1, 0, 3).reshape(cores, 9, 2 * share)
    sent = jnp.concatenate(
        [
            jnp.broadcast_to(piece, (samples, cores, lines, block)),
            jnp.broadcast_to(jnp.pad(grad_dw, ((0, 0), (0, 7), (0, 0))), (samples, cores, 16, block)),
        ],
        axis=2,
    ).reshape(peers, lines + 16, block)
    got = exchange(sent, ROWS)
    grad_pw = lax.dynamic_index_in_dim(got.reshape(samples, cores, lines + 16, block), core, 1, False)[:, :lines]
    grad_pw = grad_pw.reshape(share, 2 * outs)
    grad_dw = jnp.sum(got[:, lines : lines + 9], axis=0).reshape(9, 2, share).transpose(1, 0, 2)
    return block_out, grad_pw, grad_dw


def solution(mesh):
    samples, _ = mesh.devices.shape
    fine = Mesh(mesh.devices.reshape(samples, 8, 2, 2), ("dp", "y", "xh", "core"))
    space = ("y", "xh", "core")
    in_specs = (P("dp", space, None, None), P(), P(), P(), P("dp", space, None, None))
    out_specs = (P("dp", space, None, None), P(space, None), P(None, None, space))
    return jax.shard_map(body, mesh=fine, in_specs=in_specs, out_specs=out_specs, check_vma=False)
```

```python
import functools

import jax
import jax.numpy as jnp
from jax import lax
from jax.experimental import pallas as pl
from jax.experimental.pallas import tpu as pltpu
from jax.sharding import Mesh, PartitionSpec as P

NEAR_DILATION = 12
FAR_DILATION = 24
DILATIONS = (NEAR_DILATION, FAR_DILATION)
eps_norm = 1e-05

GROUP = ("y", "xh")
ROWS = ("dp", "core")
f32 = jnp.float32
bf16 = jnp.bfloat16


def exchange(value, axes):
    return lax.all_to_all(value, axes, 0, 0, tiled=True)


def call(kernel, name, outs, *args, scratch=(), smem=()):
    vmem = pl.BlockSpec(memory_space=pltpu.VMEM)
    specs = [pl.BlockSpec(memory_space=pltpu.SMEM) if i in smem else vmem for i in range(len(args))]
    return pl.pallas_call(
        kernel,
        name=name,
        out_shape=[jax.ShapeDtypeStruct(s, d) for s, d in outs],
        in_specs=specs,
        out_specs=[vmem] * len(outs),
        scratch_shapes=list(scratch),
    )(*args)


def pack_kernel(feat_ref, cot_ref, out_ref):
    groups, _, width = out_ref.shape
    outs = cot_ref.shape[1]
    block = width - outs
    for g in range(groups):
        out_ref[g, :, :block] = feat_ref[:, g * block : (g + 1) * block]
        out_ref[g, :, block:] = cot_ref[...]


def fill_padded(held_ref, pad):
    groups = held_ref.shape[0]
    total, rows, wide, block = pad.shape
    lead = (total - groups) // 2
    width = held_ref.shape[1] // rows
    edge = (wide - width) // 2
    for i in range(lead):
        pad[i] = jnp.zeros((rows, wide, block), f32)
        pad[lead + groups + i] = jnp.zeros((rows, wide, block), f32)

    def step(g, carry):
        value = held_ref[g, :, :block].astype(f32).reshape(rows, width, block)
        pad[lead + g, :, :edge, :] = jnp.zeros((rows, edge, block), f32)
        pad[lead + g, :, edge + width :, :] = jnp.zeros((rows, edge, block), f32)
        pad[lead + g, :, edge : edge + width, :] = value
        return carry

    lax.fori_loop(0, groups, step, 0)


def tap(pad, g, k, a, b, row_step, width, groups):
    lead = (pad.shape[0] - groups) // 2
    edge = (pad.shape[2] - width) // 2
    row = g + lead + (a - 1) * DILATIONS[k] // row_step
    col = edge + (b - 1) * DILATIONS[k]
    return pad[row, :, col : col + width, :]


def fold(value):
    lanes = value.shape[-1]
    return jnp.sum(value.reshape(-1, 8, lanes), axis=0)


def forward_kernel(row_step, held_ref, taps_ref, z_ref, sums_ref, pad):
    groups, pixels = held_ref.shape[:2]
    rows, block = pad.shape[1], pad.shape[3]
    width = pixels // rows
    fill_padded(held_ref, pad)

    def step(g, carry):
        carry = list(carry)
        for k in range(2):
            total = jnp.zeros((rows, width, block), f32)
            for a in range(3):
                for b in range(3):
                    t = 9 * k + 3 * a + b
                    total = total + taps_ref[t : t + 1, :][None] * tap(pad, g, k, a, b, row_step, width, groups)
            value = total.reshape(pixels, block).astype(bf16)
            z_ref[k, g] = value
            value = value.astype(f32)
            carry[2 * k] = carry[2 * k] + fold(value)
            carry[2 * k + 1] = carry[2 * k + 1] + fold(value * value)
        return tuple(carry)

    zero = jnp.zeros((8, block), f32)
    sums = lax.fori_loop(0, groups, step, (zero,) * 4)
    sums = [jnp.sum(s, axis=0, keepdims=True) for s in sums]
    line = lax.broadcasted_iota(jnp.int32, (8, block), 0)
    tile = zero
    for i, s in enumerate(sums):
        tile = jnp.where(line == i, s, tile)
    for i in range(sums_ref.shape[0]):
        sums_ref[i] = tile


def norm_kernel(count, z_ref, sums_ref, gain_ref, used_ref, params_ref):
    groups, block = z_ref.shape[1], z_ref.shape[3]
    sums = jnp.sum(sums_ref[...], axis=0)
    line = lax.broadcasted_iota(jnp.int32, (8, block), 0)
    tile = jnp.zeros((8, block), f32)
    stats = []
    for k in range(2):
        average = sums[2 * k : 2 * k + 1] / count
        variance = sums[2 * k + 1 : 2 * k + 2] / count - average * average
        inv = lax.rsqrt(variance + eps_norm)
        tile = jnp.where(line == 2 * k, average, tile)
        tile = jnp.where(line == 2 * k + 1, inv, tile)
        stats.append((average, inv))
    params_ref[...] = tile

    def step(g, carry):
        for k in range(2):
            average, inv = stats[k]
            xhat = (z_ref[k, g].astype(f32) - average) * inv
            scaled = gain_ref[k : k + 1, :] * xhat
            used_ref[g, :, k * block : (k + 1) * block] = jnp.maximum(scaled, 0.0).astype(bf16)
        return carry

    lax.fori_loop(0, groups, step, 0)


def back_kernel(z_ref, params_ref, gain_ref, held_ref, maps_ref, grad_ref, dxhat_ref, out_ref):
    groups, pixels, block = z_ref.shape[1:]
    params = params_ref[...]
    gain = gain_ref[...]
    zero = jnp.zeros((8, block), f32)

    def step(g, carry):
        carry = list(carry)
        back = jnp.dot(held_ref[g, :, block:], maps_ref[...], preferred_element_type=f32)
        for k in range(2):
            xhat = (z_ref[k, g].astype(f32) - params[2 * k : 2 * k + 1]) * params[2 * k + 1 : 2 * k + 2]
            scaled = gain[k : k + 1] * xhat
            dxhat = jnp.where(scaled > 0, back[:, k * block : (k + 1) * block], 0.0) * gain[k : k + 1]
            dxhat_ref[k, g] = dxhat
            carry[2 * k] = carry[2 * k] + fold(dxhat)
            carry[2 * k + 1] = carry[2 * k + 1] + fold(dxhat * xhat)
        return tuple(carry)

    sums = lax.fori_loop(0, groups, step, (zero,) * 4)
    line = lax.broadcasted_iota(jnp.int32, (8, block), 0)
    tile = zero
    for i, s in enumerate(sums):
        tile = jnp.where(line == i, jnp.sum(s, axis=0, keepdims=True), tile)
    peers, total, _ = out_ref.shape
    lines = total - 8
    cores = 2
    share = block // cores
    per = share // lines
    lanes = grad_ref.shape[1] // block
    for i in range(peers):
        j, c = divmod(i, cores)
        lane, row = divmod(j, per)
        k, lane = divmod(lane, lanes)
        top = k * block + c * share + row * lines
        out_ref[i, :lines, :] = grad_ref[top : top + lines, lane * block : (lane + 1) * block]
        out_ref[i, lines:, :] = tile


def filter_kernel(row_step, count, held_ref, z_ref, params_ref, dxhat_ref, got_ref, out_ref, pad):
    groups, pixels = held_ref.shape[:2]
    rows, block = pad.shape[1], pad.shape[3]
    width = pixels // rows
    share = block // 2
    fill_padded(held_ref, pad)
    got = jnp.sum(got_ref[...], axis=0)
    lines = got.shape[0] - 8
    seconds = got[lines:] / count
    params = params_ref[...]
    zero = jnp.zeros((8, block), f32)
    grads = []
    for k in range(2):

        def step(g, carry, k=k):
            carry = list(carry)
            xhat = (z_ref[k, g].astype(f32) - params[2 * k : 2 * k + 1]) * params[2 * k + 1 : 2 * k + 2]
            inner = dxhat_ref[k, g] - seconds[2 * k : 2 * k + 1] - xhat * seconds[2 * k + 1 : 2 * k + 2]
            dz = (params[2 * k + 1 : 2 * k + 2] * inner).astype(bf16).astype(f32).reshape(rows, width, block)
            for a in range(3):
                for b in range(3):
                    moved = tap(pad, g, k, a, b, row_step, width, groups)
                    carry[3 * a + b] = carry[3 * a + b] + fold(dz * moved)
            return tuple(carry)

        grads.append([jnp.sum(s, axis=0, keepdims=True) for s in lax.fori_loop(0, groups, step, (zero,) * 9)])
    line = lax.broadcasted_iota(jnp.int32, (16, block), 0)
    tiles = []
    for k in range(2):
        tile = jnp.zeros((16, block), f32)
        for t in range(9):
            tile = jnp.where(line == t, grads[k][t], tile)
        tiles.append(tile)
    low = lax.broadcasted_iota(jnp.int32, (16, block), 1) < share
    halves = (
        jnp.where(low, tiles[0], pltpu.roll(tiles[1], share, 1)),
        jnp.where(low, pltpu.roll(tiles[0], share, 1), tiles[1]),
    )
    for i in range(out_ref.shape[0]):
        out_ref[i, :lines, :] = got[:lines]
        out_ref[i, lines:, :] = halves[i % 2]


def mix_kernel(whole_ref, maps_ref, out_ref):
    groups, pixels, both = whole_ref.shape
    block = both // 2
    outs = out_ref.shape[1]
    total = jnp.zeros((pixels, outs), f32)
    for g in range(groups):
        for k in range(2):
            total = total + jnp.dot(
                whole_ref[g, :, k * block : (k + 1) * block],
                maps_ref[g * block : (g + 1) * block, k * outs : (k + 1) * outs],
                preferred_element_type=f32,
            )
    out_ref[...] = total.astype(bf16)


def last_kernel(core_ref, got_ref, pw_ref, dw_ref):
    peers, total, block = got_ref.shape
    share = pw_ref.shape[0]
    lines = total - 16
    per = share // lines
    core = core_ref[0]
    for j in range(peers // 2):
        lane, row = divmod(j, per)
        pw_ref[row * lines : (row + 1) * lines, lane * block : (lane + 1) * block] = got_ref[2 * j + core, :lines, :]
    dw = jnp.sum(got_ref[:, lines:, :], axis=0)
    dw_ref[0] = dw[:9, :share]
    dw_ref[1] = pltpu.roll(dw, share, 1)[:9, :share]


def body(features, depthwise, pointwise, bn_gain, cotangent):
    _, row_count, width, channels = features.shape
    outs = cotangent.shape[3]
    groups = lax.axis_size(GROUP)
    peers = lax.axis_size(ROWS)
    samples = lax.axis_size("dp")
    cores = lax.axis_size("core")
    block = channels // groups
    share = block // cores
    pixels = row_count * width
    row_step = row_count * cores
    count = float(samples * groups * cores * pixels)
    mine = lax.axis_index(GROUP)
    core = lax.axis_index("core").astype(jnp.int32).reshape(1)
    lead = FAR_DILATION // row_step
    pad = pltpu.VMEM((groups + 2 * lead, row_count, width + 2 * FAR_DILATION, block), f32)
    lines = share * 2 * outs // samples // block

    (sent,) = call(
        pack_kernel,
        "pack",
        [((groups, pixels, block + outs), bf16)],
        features.reshape(pixels, channels),
        cotangent.reshape(pixels, outs),
    )
    held = exchange(sent, GROUP)
    taps = lax.dynamic_slice_in_dim(depthwise, mine * block, block, 2).astype(f32).reshape(18, block)
    gain = lax.dynamic_slice_in_dim(bn_gain, mine * block, block, 1)
    maps = lax.dynamic_slice_in_dim(pointwise, mine * block, block, 0)
    maps = maps.reshape(block, 2, outs).transpose(2, 1, 0).reshape(outs, 2 * block)

    z, sums = call(
        functools.partial(forward_kernel, row_step),
        "forward",
        [((2, groups, pixels, block), bf16), ((peers, 8, block), f32)],
        held,
        taps,
        scratch=[pad],
    )
    sums = exchange(sums, ROWS)
    used, params = call(
        functools.partial(norm_kernel, count),
        "norm",
        [((groups, pixels, 2 * block), bf16), ((8, block), f32)],
        z,
        sums,
        gain,
    )
    whole = exchange(used, GROUP)
    grads = lax.dot_general(
        used.reshape(groups * pixels, 2 * block),
        held[:, :, block:].reshape(groups * pixels, outs),
        (((0,), (0,)), ((), ())),
        preferred_element_type=f32,
    )
    dxhat, sent = call(
        back_kernel,
        "back",
        [((2, groups, pixels, block), f32), ((peers, lines + 8, block), f32)],
        z,
        params,
        gain,
        held,
        maps,
        grads,
    )
    got = exchange(sent, ROWS)
    (sent,) = call(
        functools.partial(filter_kernel, row_step, count),
        "filter",
        [((peers, lines + 16, block), f32)],
        held,
        z,
        params,
        dxhat,
        got,
        scratch=[pad],
    )
    got = exchange(sent, ROWS)
    (block_out,) = call(mix_kernel, "mix", [((pixels, outs), bf16)], whole, pointwise)
    grad_pw, grad_dw = call(
        last_kernel, "last", [((share, 2 * outs), f32), ((2, 9, share), f32)], core, got, smem=(0,)
    )
    return block_out.reshape(1, row_count, width, outs), grad_pw, grad_dw


def solution(mesh):
    samples, _ = mesh.devices.shape
    fine = Mesh(mesh.devices.reshape(samples, 8, 2, 2), ("dp", "y", "xh", "core"))
    space = ("y", "xh", "core")
    in_specs = (P("dp", space, None, None), P(), P(), P(), P("dp", space, None, None))
    out_specs = (P("dp", space, None, None), P(space, None), P(None, None, space))
    return jax.shard_map(body, mesh=fine, in_specs=in_specs, out_specs=out_specs, check_vma=False)
```

```python
import functools

import jax
import jax.numpy as jnp
from jax import lax
from jax.experimental import pallas as pl
from jax.experimental.pallas import tpu as pltpu
from jax.sharding import Mesh, PartitionSpec as P

NEAR_DILATION = 12
FAR_DILATION = 24
DILATIONS = (NEAR_DILATION, FAR_DILATION)
eps_norm = 1e-05

GROUP = ("y", "xh")
ORDER = (0, -1, 1, -2, 2, -3, 3, -4)
ROWS = ("dp", "core")
f32 = jnp.float32
bf16 = jnp.bfloat16


def exchange(value, axes):
    return lax.all_to_all(value, axes, 0, 0, tiled=True)


def shifted(value, steps):
    count = lax.axis_size("y")
    return lax.ppermute(value, "y", [(i, (i + steps) % count) for i in range(count)])


def call(kernel, name, outs, *args, scratch=(), smem=()):
    vmem = pl.BlockSpec(memory_space=pltpu.VMEM)
    specs = [pl.BlockSpec(memory_space=pltpu.SMEM) if i in smem else vmem for i in range(len(args))]
    return pl.pallas_call(
        kernel,
        name=name,
        out_shape=[jax.ShapeDtypeStruct(s, d) for s, d in outs],
        in_specs=specs,
        out_specs=[vmem] * len(outs),
        scratch_shapes=list(scratch),
    )(*args)


def pack_kernel(feat_ref, out_ref):
    groups, _, block = out_ref.shape
    for g in range(groups):
        out_ref[g] = feat_ref[:, g * block : (g + 1) * block]


def fill_padded(held_ref, pad):
    groups = held_ref.shape[0]
    total, rows, wide, block = pad.shape
    lead = (total - groups) // 2
    width = held_ref.shape[1] // rows
    edge = (wide - width) // 2
    for i in range(lead):
        pad[i] = jnp.zeros((rows, wide, block), f32)
        pad[lead + groups + i] = jnp.zeros((rows, wide, block), f32)

    def step(g, carry):
        value = held_ref[g].astype(f32).reshape(rows, width, block)
        pad[lead + g, :, :edge, :] = jnp.zeros((rows, edge, block), f32)
        pad[lead + g, :, edge + width :, :] = jnp.zeros((rows, edge, block), f32)
        pad[lead + g, :, edge : edge + width, :] = value
        return carry

    lax.fori_loop(0, groups, step, 0)


def tap(pad, g, k, a, b, row_step, width, groups):
    lead = (pad.shape[0] - groups) // 2
    edge = (pad.shape[2] - width) // 2
    row = g + lead + (a - 1) * DILATIONS[k] // row_step
    col = edge + (b - 1) * DILATIONS[k]
    return pad[row, :, col : col + width, :]


def fold(value):
    lanes = value.shape[-1]
    return jnp.sum(value.reshape(-1, 8, lanes), axis=0)


def forward_kernel(row_step, held_ref, taps_ref, z_ref, sums_ref, pad):
    groups, pixels = held_ref.shape[:2]
    rows, block = pad.shape[1], pad.shape[3]
    width = pixels // rows
    fill_padded(held_ref, pad)

    def step(g, carry):
        carry = list(carry)
        for k in range(2):
            total = jnp.zeros((rows, width, block), f32)
            for a in range(3):
                for b in range(3):
                    t = 9 * k + 3 * a + b
                    total = total + taps_ref[t : t + 1, :][None] * tap(pad, g, k, a, b, row_step, width, groups)
            value = total.reshape(pixels, block).astype(bf16)
            z_ref[k, g] = value
            value = value.astype(f32)
            carry[2 * k] = carry[2 * k] + fold(value)
            carry[2 * k + 1] = carry[2 * k + 1] + fold(value * value)
        return tuple(carry)

    zero = jnp.zeros((8, block), f32)
    sums = lax.fori_loop(0, groups, step, (zero,) * 4)
    sums = [jnp.sum(s, axis=0, keepdims=True) for s in sums]
    line = lax.broadcasted_iota(jnp.int32, (8, block), 0)
    tile = zero
    for i, s in enumerate(sums):
        tile = jnp.where(line == i, s, tile)
    for i in range(sums_ref.shape[0]):
        sums_ref[i] = tile


def norm_kernel(count, z_ref, sums_ref, gain_ref, used_ref, params_ref):
    groups, block = z_ref.shape[1], z_ref.shape[3]
    sums = jnp.sum(sums_ref[...], axis=0)
    line = lax.broadcasted_iota(jnp.int32, (8, block), 0)
    tile = jnp.zeros((8, block), f32)
    stats = []
    for k in range(2):
        average = sums[2 * k : 2 * k + 1] / count
        variance = sums[2 * k + 1 : 2 * k + 2] / count - average * average
        inv = lax.rsqrt(variance + eps_norm)
        tile = jnp.where(line == 2 * k, average, tile)
        tile = jnp.where(line == 2 * k + 1, inv, tile)
        stats.append((average, inv))
    params_ref[...] = tile

    def step(g, carry):
        for k in range(2):
            average, inv = stats[k]
            xhat = (z_ref[k, g].astype(f32) - average) * inv
            scaled = gain_ref[k : k + 1, :] * xhat
            used_ref[g, :, k * block : (k + 1) * block] = jnp.maximum(scaled, 0.0).astype(bf16)
        return carry

    lax.fori_loop(0, groups, step, 0)


def back_kernel(place_ref, z_ref, params_ref, gain_ref, *refs):
    *pair_refs, maps_ref, dxhat_ref, out_ref, total_ref, cots_ref = refs
    _, groups, pixels, block = z_ref.shape
    params = params_ref[...]
    gain = gain_ref[...]
    rows, half = len(pair_refs), place_ref[1]
    zero = jnp.zeros((8, block), f32)
    total_ref[...] = jnp.zeros_like(total_ref)
    for apart, ref in zip(ORDER, pair_refs, strict=True):
        row = (place_ref[0] + apart + rows) % rows
        for slot in range(2):
            cots_ref[2 * row + (half ^ slot)] = ref[slot]
    if True:

        def step(g, carry):
            carry = list(carry)
            cot = cots_ref[g]
            back = jnp.dot(cot, maps_ref[...], preferred_element_type=f32)
            used = []
            for k in range(2):
                xhat = (z_ref[k, g].astype(f32) - params[2 * k : 2 * k + 1]) * params[2 * k + 1 : 2 * k + 2]
                scaled = gain[k : k + 1] * xhat
                used.append(jnp.maximum(scaled, 0.0).astype(bf16))
                dxhat = jnp.where(scaled > 0, back[:, k * block : (k + 1) * block], 0.0) * gain[k : k + 1]
                dxhat_ref[k, g] = dxhat
                carry[2 * k] = carry[2 * k] + fold(dxhat)
                carry[2 * k + 1] = carry[2 * k + 1] + fold(dxhat * xhat)
            for k in range(2):
                total_ref[k * block : (k + 1) * block, :] += lax.dot_general(
                    used[k], cot, (((0,), (0,)), ((), ())), preferred_element_type=f32
                )
            return tuple(carry)

        sums = lax.fori_loop(0, groups, step, (zero,) * 4)
    line = lax.broadcasted_iota(jnp.int32, (8, block), 0)
    tile = zero
    for i, s in enumerate(sums):
        tile = jnp.where(line == i, jnp.sum(s, axis=0, keepdims=True), tile)
    peers, total, _ = out_ref.shape
    lines = total - 8
    cores = 2
    share = block // cores
    per = share // lines
    lanes = total_ref.shape[1] // block
    for i in range(peers):
        j, c = divmod(i, cores)
        lane, row = divmod(j, per)
        k, lane = divmod(lane, lanes)
        top = k * block + c * share + row * lines
        out_ref[i, :lines, :] = total_ref[top : top + lines, lane * block : (lane + 1) * block]
        out_ref[i, lines:, :] = tile


def filter_kernel(row_step, count, held_ref, z_ref, params_ref, dxhat_ref, got_ref, out_ref, pad):
    groups, pixels = held_ref.shape[:2]
    rows, block = pad.shape[1], pad.shape[3]
    width = pixels // rows
    share = block // 2
    fill_padded(held_ref, pad)
    got = jnp.sum(got_ref[...], axis=0)
    lines = got.shape[0] - 8
    seconds = got[lines:] / count
    params = params_ref[...]
    zero = jnp.zeros((8, block), f32)
    grads = []
    for k in range(2):

        def step(g, carry, k=k):
            carry = list(carry)
            xhat = (z_ref[k, g].astype(f32) - params[2 * k : 2 * k + 1]) * params[2 * k + 1 : 2 * k + 2]
            inner = dxhat_ref[k, g] - seconds[2 * k : 2 * k + 1] - xhat * seconds[2 * k + 1 : 2 * k + 2]
            dz = (params[2 * k + 1 : 2 * k + 2] * inner).astype(bf16).astype(f32).reshape(rows, width, block)
            for a in range(3):
                for b in range(3):
                    moved = tap(pad, g, k, a, b, row_step, width, groups)
                    carry[3 * a + b] = carry[3 * a + b] + fold(dz * moved)
            return tuple(carry)

        grads.append([jnp.sum(s, axis=0, keepdims=True) for s in lax.fori_loop(0, groups, step, (zero,) * 9)])
    line = lax.broadcasted_iota(jnp.int32, (16, block), 0)
    tiles = []
    for k in range(2):
        tile = jnp.zeros((16, block), f32)
        for t in range(9):
            tile = jnp.where(line == t, grads[k][t], tile)
        tiles.append(tile)
    low = lax.broadcasted_iota(jnp.int32, (16, block), 1) < share
    halves = (
        jnp.where(low, tiles[0], pltpu.roll(tiles[1], share, 1)),
        jnp.where(low, pltpu.roll(tiles[0], share, 1), tiles[1]),
    )
    for i in range(out_ref.shape[0]):
        out_ref[i, :lines, :] = got[:lines]
        out_ref[i, lines:, :] = halves[i % 2]


def mix_kernel(whole_ref, maps_ref, out_ref):
    groups, pixels, both = whole_ref.shape
    block = both // 2
    outs = out_ref.shape[1]
    total = jnp.zeros((pixels, outs), f32)
    for g in range(groups):
        for k in range(2):
            total = total + jnp.dot(
                whole_ref[g, :, k * block : (k + 1) * block],
                maps_ref[g * block : (g + 1) * block, k * outs : (k + 1) * outs],
                preferred_element_type=f32,
            )
    out_ref[...] = total.astype(bf16)


def last_kernel(core_ref, got_ref, pw_ref, dw_ref):
    peers, total, block = got_ref.shape
    share = pw_ref.shape[0]
    lines = total - 16
    per = share // lines
    core = core_ref[0]
    for j in range(peers // 2):
        lane, row = divmod(j, per)
        pw_ref[row * lines : (row + 1) * lines, lane * block : (lane + 1) * block] = got_ref[2 * j + core, :lines, :]
    dw = jnp.sum(got_ref[:, lines:, :], axis=0)
    dw_ref[0] = dw[:9, :share]
    dw_ref[1] = pltpu.roll(dw, share, 1)[:9, :share]


def body(features, depthwise, pointwise, bn_gain, cotangent):
    _, row_count, width, channels = features.shape
    outs = cotangent.shape[3]
    groups = lax.axis_size(GROUP)
    peers = lax.axis_size(ROWS)
    samples = lax.axis_size("dp")
    cores = lax.axis_size("core")
    block = channels // groups
    share = block // cores
    pixels = row_count * width
    row_step = row_count * cores
    count = float(samples * groups * cores * pixels)
    mine = lax.axis_index(GROUP)
    core = lax.axis_index("core").astype(jnp.int32).reshape(1)
    lead = FAR_DILATION // row_step
    pad = pltpu.VMEM((groups + 2 * lead, row_count, width + 2 * FAR_DILATION, block), f32)
    lines = share * 2 * outs // samples // block

    (sent,) = call(pack_kernel, "pack", [((groups, pixels, block), bf16)], features.reshape(pixels, channels))
    held = exchange(sent, GROUP)
    cot = cotangent.reshape(1, pixels, outs)
    pairs = [jnp.concatenate([cot, lax.ppermute(cot, "xh", [(0, 1), (1, 0)])], axis=0)]
    left = right = pairs[0]
    for hop in range(2):
        left, right = shifted(left, 1), shifted(right, -1)
        pairs += [left, right]
    held, left, right = lax.optimization_barrier((held, left, right))
    left, right = shifted(left, 1), shifted(right, -1)
    pairs += [left, right, shifted(left, 1)]
    taps = lax.dynamic_slice_in_dim(depthwise, mine * block, block, 2).astype(f32).reshape(18, block)
    gain = lax.dynamic_slice_in_dim(bn_gain, mine * block, block, 1)
    maps = lax.dynamic_slice_in_dim(pointwise, mine * block, block, 0)
    maps = maps.reshape(block, 2, outs).transpose(2, 1, 0).reshape(outs, 2 * block)

    z, sums = call(
        functools.partial(forward_kernel, row_step),
        "forward",
        [((2, groups, pixels, block), bf16), ((peers, 8, block), f32)],
        held,
        taps,
        scratch=[pad],
    )
    sums = exchange(sums, ROWS)
    sums, *pairs = lax.optimization_barrier((sums, *pairs))
    used, params = call(
        functools.partial(norm_kernel, count),
        "norm",
        [((groups, pixels, 2 * block), bf16), ((8, block), f32)],
        z,
        sums,
        gain,
    )
    whole = exchange(used, GROUP)
    dxhat, sent = call(
        back_kernel,
        "back",
        [((2, groups, pixels, block), f32), ((peers, lines + 8, block), f32)],
        jnp.stack([lax.axis_index("y"), lax.axis_index("xh")]).astype(jnp.int32),
        z,
        params,
        gain,
        *pairs,
        maps,
        scratch=[pltpu.VMEM((2 * block, outs), f32), pltpu.VMEM((groups, pixels, outs), bf16)],
        smem=(0,),
    )
    whole, sent = lax.optimization_barrier((whole, sent))
    got = exchange(sent, ROWS)
    (sent,) = call(
        functools.partial(filter_kernel, row_step, count),
        "filter",
        [((peers, lines + 16, block), f32)],
        held,
        z,
        params,
        dxhat,
        got,
        scratch=[pad],
    )
    got = exchange(sent, ROWS)
    (block_out,) = call(mix_kernel, "mix", [((pixels, outs), bf16)], whole, pointwise)
    grad_pw, grad_dw = call(
        last_kernel, "last", [((share, 2 * outs), f32), ((2, 9, share), f32)], core, got, smem=(0,)
    )
    return block_out.reshape(1, row_count, width, outs), grad_pw, grad_dw


def solution(mesh):
    samples, _ = mesh.devices.shape
    fine = Mesh(mesh.devices.reshape(samples, 8, 2, 2), ("dp", "y", "xh", "core"))
    space = ("y", "xh", "core")
    in_specs = (P("dp", space, None, None), P(), P(), P(), P("dp", space, None, None))
    out_specs = (P("dp", space, None, None), P(space, None), P(None, None, space))
    return jax.shard_map(body, mesh=fine, in_specs=in_specs, out_specs=out_specs, check_vma=False)
```

```python
import functools

import jax
import jax.numpy as jnp
from jax import lax
from jax.experimental import pallas as pl
from jax.experimental.pallas import tpu as pltpu
from jax.sharding import Mesh, PartitionSpec as P

NEAR_DILATION = 12
FAR_DILATION = 24
DILATIONS = (NEAR_DILATION, FAR_DILATION)
eps_norm = 1e-05

GROUP = ("y", "xh")
ORDER = (0, -1, 1, -2, 2, -3, 3, -4)
ROWS = ("dp", "core")
f32 = jnp.float32
bf16 = jnp.bfloat16


def exchange(value, axes):
    return lax.all_to_all(value, axes, 0, 0, tiled=True)


def shifted(value, steps):
    count = lax.axis_size("y")
    return lax.ppermute(value, "y", [(i, (i + steps) % count) for i in range(count)])


def call(kernel, name, outs, *args, scratch=(), smem=(), slow=()):
    vmem = pl.BlockSpec(memory_space=pltpu.VMEM)
    specs = [pl.BlockSpec(memory_space=pltpu.SMEM) if i in smem else vmem for i in range(len(args))]
    args = [
        pltpu.with_memory_space_constraint(a, pltpu.HBM) if i in slow else a for i, a in enumerate(args)
    ]
    return pl.pallas_call(
        kernel,
        name=name,
        out_shape=[pltpu.HBM(*o[:2]) if len(o) == 3 else jax.ShapeDtypeStruct(*o) for o in outs],
        in_specs=specs,
        out_specs=[vmem] * len(outs),
        scratch_shapes=list(scratch),
        compiler_params=pltpu.CompilerParams(vmem_limit_bytes=24 << 20),
    )(*args)


def pack_kernel(feat_ref, out_ref):
    groups, _, block = out_ref.shape
    for g in range(groups):
        out_ref[g] = feat_ref[:, g * block : (g + 1) * block]


def fill_padded(held_ref, pad):
    groups = held_ref.shape[0]
    total, rows, wide, block = pad.shape
    lead = (total - groups) // 2
    width = held_ref.shape[1] // rows
    edge = (wide - width) // 2
    for i in range(lead):
        pad[i] = jnp.zeros((rows, wide, block), f32)
        pad[lead + groups + i] = jnp.zeros((rows, wide, block), f32)

    def step(g, carry):
        value = held_ref[g].astype(f32).reshape(rows, width, block)
        pad[lead + g, :, :edge, :] = jnp.zeros((rows, edge, block), f32)
        pad[lead + g, :, edge + width :, :] = jnp.zeros((rows, edge, block), f32)
        pad[lead + g, :, edge : edge + width, :] = value
        return carry

    lax.fori_loop(0, groups, step, 0)


def tap(pad, g, k, a, b, row_step, width, groups):
    lead = (pad.shape[0] - groups) // 2
    edge = (pad.shape[2] - width) // 2
    row = g + lead + (a - 1) * DILATIONS[k] // row_step
    col = edge + (b - 1) * DILATIONS[k]
    return pad[row, :, col : col + width, :]


def fold(value):
    lanes = value.shape[-1]
    return jnp.sum(value.reshape(-1, 8, lanes), axis=0)


def forward_kernel(row_step, held_ref, taps_ref, z_ref, sums_ref, pad):
    groups, pixels = held_ref.shape[:2]
    rows, block = pad.shape[1], pad.shape[3]
    width = pixels // rows
    fill_padded(held_ref, pad)

    def step(g, carry):
        carry = list(carry)
        for k in range(2):
            total = jnp.zeros((rows, width, block), f32)
            for a in range(3):
                for b in range(3):
                    t = 9 * k + 3 * a + b
                    total = total + taps_ref[t : t + 1, :][None] * tap(pad, g, k, a, b, row_step, width, groups)
            value = total.reshape(pixels, block).astype(bf16)
            z_ref[k, g] = value
            value = value.astype(f32)
            carry[2 * k] = carry[2 * k] + fold(value)
            carry[2 * k + 1] = carry[2 * k + 1] + fold(value * value)
        return tuple(carry)

    zero = jnp.zeros((8, block), f32)
    sums = lax.fori_loop(0, groups, step, (zero,) * 4)
    sums = [jnp.sum(s, axis=0, keepdims=True) for s in sums]
    line = lax.broadcasted_iota(jnp.int32, (8, block), 0)
    tile = zero
    for i, s in enumerate(sums):
        tile = jnp.where(line == i, s, tile)
    for i in range(sums_ref.shape[0]):
        sums_ref[i] = tile


def norm_kernel(count, z_ref, sums_ref, gain_ref, used_ref, params_ref):
    groups, block = z_ref.shape[1], z_ref.shape[3]
    sums = jnp.sum(sums_ref[...], axis=0)
    line = lax.broadcasted_iota(jnp.int32, (8, block), 0)
    tile = jnp.zeros((8, block), f32)
    stats = []
    for k in range(2):
        average = sums[2 * k : 2 * k + 1] / count
        variance = sums[2 * k + 1 : 2 * k + 2] / count - average * average
        inv = lax.rsqrt(variance + eps_norm)
        tile = jnp.where(line == 2 * k, average, tile)
        tile = jnp.where(line == 2 * k + 1, inv, tile)
        stats.append((average, inv))
    params_ref[...] = tile

    def step(g, carry):
        for k in range(2):
            average, inv = stats[k]
            xhat = (z_ref[k, g].astype(f32) - average) * inv
            scaled = gain_ref[k : k + 1, :] * xhat
            used_ref[g, :, k * block : (k + 1) * block] = jnp.maximum(scaled, 0.0).astype(bf16)
        return carry

    lax.fori_loop(0, groups, step, 0)


def place_of(i, peers, lanes):
    per = peers // (2 * lanes)
    return i // (per * lanes), i // per % lanes, i % per


def back_kernel(place_ref, z_ref, params_ref, gain_ref, *refs):
    *pair_refs, maps_ref, dxhat_ref, out_ref, total_ref, cots_ref = refs
    _, groups, pixels, block = z_ref.shape
    params = params_ref[...]
    gain = gain_ref[...]
    rows, half = len(pair_refs), place_ref[1]
    zero = jnp.zeros((8, block), f32)
    total_ref[...] = jnp.zeros_like(total_ref)
    for apart, ref in zip(ORDER, pair_refs, strict=True):
        row = (place_ref[0] + apart + rows) % rows
        for slot in range(2):
            cots_ref[2 * row + (half ^ slot)] = ref[slot]
    if True:

        def step(g, carry):
            carry = list(carry)
            cot = cots_ref[g]
            back = jnp.dot(cot, maps_ref[...], preferred_element_type=f32)
            used = []
            for k in range(2):
                xhat = (z_ref[k, g].astype(f32) - params[2 * k : 2 * k + 1]) * params[2 * k + 1 : 2 * k + 2]
                scaled = gain[k : k + 1] * xhat
                used.append(jnp.maximum(scaled, 0.0).astype(bf16))
                dxhat = jnp.where(scaled > 0, back[:, k * block : (k + 1) * block], 0.0) * gain[k : k + 1]
                dxhat_ref[k, g] = dxhat
                carry[2 * k] = carry[2 * k] + fold(dxhat)
                carry[2 * k + 1] = carry[2 * k + 1] + fold(dxhat * xhat)
            for k in range(2):
                total_ref[k * block : (k + 1) * block, :] += lax.dot_general(
                    used[k], cot, (((0,), (0,)), ((), ())), preferred_element_type=f32
                )
            return tuple(carry)

        sums = lax.fori_loop(0, groups, step, (zero,) * 4)
    line = lax.broadcasted_iota(jnp.int32, (8, block), 0)
    tile = zero
    for i, s in enumerate(sums):
        tile = jnp.where(line == i, jnp.sum(s, axis=0, keepdims=True), tile)
    peers, total, _ = out_ref.shape
    lines = (total - 8) // 2
    share = block // 2
    for i in range(peers):
        k, lane, row = place_of(i, peers, total_ref.shape[1] // block)
        for c in range(2):
            top = k * block + c * share + row * lines
            out_ref[i, c * lines : (c + 1) * lines, :] = total_ref[top : top + lines, lane * block : (lane + 1) * block]
        out_ref[i, 2 * lines :, :] = tile


def filter_kernel(row_step, count, held_ref, z_ref, params_ref, dxhat_ref, got_ref, out_ref, pad):
    groups, pixels = held_ref.shape[:2]
    rows, block = pad.shape[1], pad.shape[3]
    width = pixels // rows
    share = block // 2
    fill_padded(held_ref, pad)
    got = jnp.sum(got_ref[...], axis=0)
    lines = (got.shape[0] - 8) // 2
    seconds = got[2 * lines :] / count
    params = params_ref[...]
    zero = jnp.zeros((8, block), f32)
    grads = []
    for k in range(2):

        def step(g, carry, k=k):
            carry = list(carry)
            xhat = (z_ref[k, g].astype(f32) - params[2 * k : 2 * k + 1]) * params[2 * k + 1 : 2 * k + 2]
            inner = dxhat_ref[k, g] - seconds[2 * k : 2 * k + 1] - xhat * seconds[2 * k + 1 : 2 * k + 2]
            dz = (params[2 * k + 1 : 2 * k + 2] * inner).astype(bf16).astype(f32).reshape(rows, width, block)
            for a in range(3):
                for b in range(3):
                    moved = tap(pad, g, k, a, b, row_step, width, groups)
                    carry[3 * a + b] = carry[3 * a + b] + fold(dz * moved)
            return tuple(carry)

        grads.append([jnp.sum(s, axis=0, keepdims=True) for s in lax.fori_loop(0, groups, step, (zero,) * 9)])
    line = lax.broadcasted_iota(jnp.int32, (16, block), 0)
    tiles = []
    for k in range(2):
        tile = jnp.zeros((16, block), f32)
        for t in range(9):
            tile = jnp.where(line == t, grads[k][t], tile)
        tiles.append(tile)
    low = lax.broadcasted_iota(jnp.int32, (16, block), 1) < share
    halves = (
        jnp.where(low, tiles[0], pltpu.roll(tiles[1], share, 1)),
        jnp.where(low, pltpu.roll(tiles[0], share, 1), tiles[1]),
    )
    for i in range(out_ref.shape[0]):
        out_ref[i, :lines, :] = got[i % 2 * lines : (i % 2 + 1) * lines]
        out_ref[i, lines:, :] = halves[i % 2]


def mix_kernel(whole_ref, maps_ref, out_ref):
    groups, pixels, both = whole_ref.shape
    block = both // 2
    outs = out_ref.shape[1]
    total = jnp.zeros((pixels, outs), f32)
    for g in range(groups):
        for k in range(2):
            total = total + jnp.dot(
                whole_ref[g, :, k * block : (k + 1) * block],
                maps_ref[g * block : (g + 1) * block, k * outs : (k + 1) * outs],
                preferred_element_type=f32,
            )
    out_ref[...] = total.astype(bf16)


def last_kernel(got_ref, pw_ref, dw_ref):
    peers, total, block = got_ref.shape
    share, wide = pw_ref.shape
    lines = total - 16
    lanes = wide // 2 // block
    for i in range(peers):
        k, lane, row = place_of(i, peers, lanes)
        left = (k * lanes + lane) * block
        pw_ref[row * lines : (row + 1) * lines, left : left + block] = got_ref[i, :lines, :]
    dw = jnp.sum(got_ref[:, lines:, :], axis=0)
    dw_ref[0] = dw[:9, :share]
    dw_ref[1] = pltpu.roll(dw, share, 1)[:9, :share]


def body(features, depthwise, pointwise, bn_gain, cotangent):
    _, row_count, width, channels = features.shape
    outs = cotangent.shape[3]
    groups = lax.axis_size(GROUP)
    peers = lax.axis_size(ROWS)
    samples = lax.axis_size("dp")
    cores = lax.axis_size("core")
    block = channels // groups
    share = block // cores
    pixels = row_count * width
    row_step = row_count * cores
    count = float(samples * groups * cores * pixels)
    mine = lax.axis_index(GROUP)
    lead = FAR_DILATION // row_step
    pad = pltpu.VMEM((groups + 2 * lead, row_count, width + 2 * FAR_DILATION, block), f32)
    lines = share * 2 * outs // peers // block

    (sent,) = call(pack_kernel, "pack", [((groups, pixels, block), bf16, None)], features.reshape(pixels, channels), slow=(0,))
    held = exchange(sent, GROUP)
    cot = cotangent.reshape(1, pixels, outs)
    pairs = [jnp.concatenate([cot, lax.ppermute(cot, "xh", [(0, 1), (1, 0)])], axis=0)]
    left, right = shifted(pairs[0], 1), shifted(pairs[0], -1)
    held, left, right = lax.optimization_barrier((held, left, right))
    pairs += [left, right]
    for hop in range(2):
        left, right = shifted(left, 1), shifted(right, -1)
        pairs += [left, right]
    pairs.append(shifted(left, 1))
    taps = lax.dynamic_slice_in_dim(depthwise, mine * block, block, 2).astype(f32).reshape(18, block)
    gain = lax.dynamic_slice_in_dim(bn_gain, mine * block, block, 1)
    maps = lax.dynamic_slice_in_dim(pointwise, mine * block, block, 0)
    maps = maps.reshape(block, 2, outs).transpose(2, 1, 0).reshape(outs, 2 * block)

    z, sums = call(
        functools.partial(forward_kernel, row_step),
        "forward",
        [((2, groups, pixels, block), bf16), ((peers, 8, block), f32, None)],
        held,
        taps,
        scratch=[pad],
    )
    sums = exchange(sums, ROWS)
    sums, *pairs = lax.optimization_barrier((sums, *pairs))
    used, params = call(
        functools.partial(norm_kernel, count),
        "norm",
        [((groups, pixels, 2 * block), bf16, None), ((8, block), f32)],
        z,
        sums,
        gain,
    )
    whole = exchange(used, GROUP)
    dxhat, sent = call(
        back_kernel,
        "back",
        [((2, groups, pixels, block), f32, None), ((peers, 2 * lines + 8, block), f32, None)],
        jnp.stack([lax.axis_index("y"), lax.axis_index("xh")]).astype(jnp.int32),
        z,
        params,
        gain,
        *pairs,
        maps,
        slow=range(4, 4 + len(pairs)),
        scratch=[pltpu.VMEM((2 * block, outs), f32), pltpu.VMEM((groups, pixels, outs), bf16)],
        smem=(0,),
    )
    whole, sent = lax.optimization_barrier((whole, sent))
    got = exchange(sent, ROWS)
    (sent,) = call(
        functools.partial(filter_kernel, row_step, count),
        "filter",
        [((peers, lines + 16, block), f32, None)],
        held,
        z,
        params,
        dxhat,
        got,
        slow=(3,),
        scratch=[pad],
    )
    got = exchange(sent, ROWS)
    (block_out,) = call(mix_kernel, "mix", [((pixels, outs), bf16, None)], whole, pointwise, slow=(1,))
    grad_pw, grad_dw = call(
        last_kernel, "last", [((share, 2 * outs), f32, None), ((2, 9, share), f32, None)], got
    )
    return block_out.reshape(1, row_count, width, outs), grad_pw, grad_dw


def solution(mesh):
    samples, _ = mesh.devices.shape
    fine = Mesh(mesh.devices.reshape(samples, 8, 2, 2), ("dp", "y", "xh", "core"))
    space = ("y", "xh", "core")
    in_specs = (P("dp", space, None, None), P(), P(), P(), P("dp", space, None, None))
    out_specs = (P("dp", space, None, None), P(space, None), P(None, None, space))
    return jax.shard_map(body, mesh=fine, in_specs=in_specs, out_specs=out_specs, check_vma=False)
```

```python
import functools

import jax
import jax.numpy as jnp
from jax import lax
from jax.experimental import pallas as pl
from jax.experimental.pallas import tpu as pltpu
from jax.sharding import Mesh, PartitionSpec as P

NEAR_DILATION = 12
FAR_DILATION = 24
DILATIONS = (NEAR_DILATION, FAR_DILATION)
eps_norm = 1e-05

GROUP = ("y", "xh")
ORDER = ((-1, 0, 1), (-4, -3, -2), (2, 3))
DP = ("z", "xl")
ROWS = ("z", "xl", "core")
f32 = jnp.float32
bf16 = jnp.bfloat16


def exchange(value, axes):
    return lax.all_to_all(value, axes, 0, 0, tiled=True)


def shifted(value, steps):
    count = lax.axis_size("y")
    return lax.ppermute(value, "y", [(i, (i + steps) % count) for i in range(count)])


def call(kernel, name, outs, *args, scratch=(), smem=(), slow=()):
    vmem = pl.BlockSpec(memory_space=pltpu.VMEM)
    specs = [pl.BlockSpec(memory_space=pltpu.SMEM) if i in smem else vmem for i in range(len(args))]
    args = [
        pltpu.with_memory_space_constraint(a, pltpu.HBM) if i in slow else a for i, a in enumerate(args)
    ]
    return pl.pallas_call(
        kernel,
        name=name,
        out_shape=[pltpu.HBM(*o[:2]) if len(o) == 3 else jax.ShapeDtypeStruct(*o) for o in outs],
        in_specs=specs,
        out_specs=[vmem] * len(outs),
        scratch_shapes=list(scratch),
        compiler_params=pltpu.CompilerParams(vmem_limit_bytes=24 << 20),
    )(*args)


def pack_kernel(feat_ref, out_ref):
    groups, _, block = out_ref.shape
    for g in range(groups):
        out_ref[g] = feat_ref[:, g * block : (g + 1) * block]


def fill_padded(held_ref, pad):
    groups = held_ref.shape[0]
    total, rows, wide, block = pad.shape
    lead = (total - groups) // 2
    width = held_ref.shape[1] // rows
    edge = (wide - width) // 2
    for i in range(lead):
        pad[i] = jnp.zeros((rows, wide, block), f32)
        pad[lead + groups + i] = jnp.zeros((rows, wide, block), f32)

    def step(g, carry):
        value = held_ref[g].astype(f32).reshape(rows, width, block)
        pad[lead + g, :, :edge, :] = jnp.zeros((rows, edge, block), f32)
        pad[lead + g, :, edge + width :, :] = jnp.zeros((rows, edge, block), f32)
        pad[lead + g, :, edge : edge + width, :] = value
        return carry

    lax.fori_loop(0, groups, step, 0)


def tap(pad, g, k, a, b, row_step, width, groups):
    lead = (pad.shape[0] - groups) // 2
    edge = (pad.shape[2] - width) // 2
    row = g + lead + (a - 1) * DILATIONS[k] // row_step
    col = edge + (b - 1) * DILATIONS[k]
    return pad[row, :, col : col + width, :]


def fold(value):
    lanes = value.shape[-1]
    return jnp.sum(value.reshape(-1, 8, lanes), axis=0)


def forward_kernel(row_step, held_ref, taps_ref, z_ref, sums_ref, pad):
    groups, pixels = held_ref.shape[:2]
    rows, block = pad.shape[1], pad.shape[3]
    width = pixels // rows
    fill_padded(held_ref, pad)

    def step(g, carry):
        carry = list(carry)
        for k in range(2):
            total = jnp.zeros((rows, width, block), f32)
            for a in range(3):
                for b in range(3):
                    t = 9 * k + 3 * a + b
                    total = total + taps_ref[t : t + 1, :][None] * tap(pad, g, k, a, b, row_step, width, groups)
            value = total.reshape(pixels, block).astype(bf16)
            z_ref[k, g] = value
            value = value.astype(f32)
            carry[2 * k] = carry[2 * k] + fold(value)
            carry[2 * k + 1] = carry[2 * k + 1] + fold(value * value)
        return tuple(carry)

    zero = jnp.zeros((8, block), f32)
    sums = lax.fori_loop(0, groups, step, (zero,) * 4)
    sums = [jnp.sum(s, axis=0, keepdims=True) for s in sums]
    line = lax.broadcasted_iota(jnp.int32, (8, block), 0)
    tile = zero
    for i, s in enumerate(sums):
        tile = jnp.where(line == i, s, tile)
    for i in range(sums_ref.shape[0]):
        sums_ref[i] = tile


def norm_kernel(count, z_ref, sums_ref, gain_ref, used_ref, params_ref):
    groups, block = z_ref.shape[1], z_ref.shape[3]
    sums = jnp.sum(sums_ref[...], axis=0)
    line = lax.broadcasted_iota(jnp.int32, (8, block), 0)
    tile = jnp.zeros((8, block), f32)
    stats = []
    for k in range(2):
        average = sums[2 * k : 2 * k + 1] / count
        variance = sums[2 * k + 1 : 2 * k + 2] / count - average * average
        inv = lax.rsqrt(variance + eps_norm)
        tile = jnp.where(line == 2 * k, average, tile)
        tile = jnp.where(line == 2 * k + 1, inv, tile)
        stats.append((average, inv))
    params_ref[...] = tile

    def step(g, carry):
        for k in range(2):
            average, inv = stats[k]
            xhat = (z_ref[k, g].astype(f32) - average) * inv
            scaled = gain_ref[k : k + 1, :] * xhat
            used_ref[g, :, k * block : (k + 1) * block] = jnp.maximum(scaled, 0.0).astype(bf16)
        return carry

    lax.fori_loop(0, groups, step, 0)


def place_of(i):
    return i % 2, i // 2 % 2, i // 4


def back_kernel(place_ref, z_ref, params_ref, gain_ref, *refs):
    *pair_refs, maps_ref, dxhat_ref, keep_ref, send_ref, total_ref, cots_ref = refs
    _, groups, pixels, block = z_ref.shape
    params = params_ref[...]
    gain = gain_ref[...]
    rows, half = groups // 2, place_ref[1]
    zero = jnp.zeros((8, block), f32)
    total_ref[...] = jnp.zeros_like(total_ref)
    for aparts, ref in zip(ORDER, pair_refs, strict=True):
        for i, apart in enumerate(aparts):
            row = (place_ref[0] + apart + rows) % rows
            for slot in range(2):
                cots_ref[2 * row + (half ^ slot)] = ref[2 * i + slot]
    if True:

        def step(g, carry):
            carry = list(carry)
            cot = cots_ref[g]
            back = jnp.dot(cot, maps_ref[...], preferred_element_type=f32)
            used = []
            for k in range(2):
                xhat = (z_ref[k, g].astype(f32) - params[2 * k : 2 * k + 1]) * params[2 * k + 1 : 2 * k + 2]
                scaled = gain[k : k + 1] * xhat
                used.append(jnp.maximum(scaled, 0.0).astype(bf16))
                dxhat = jnp.where(scaled > 0, back[:, k * block : (k + 1) * block], 0.0) * gain[k : k + 1]
                dxhat_ref[k, g] = dxhat
                carry[2 * k] = carry[2 * k] + fold(dxhat)
                carry[2 * k + 1] = carry[2 * k + 1] + fold(dxhat * xhat)
            for k in range(2):
                total_ref[k * block : (k + 1) * block, :] += lax.dot_general(
                    used[k], cot, (((0,), (0,)), ((), ())), preferred_element_type=f32
                )
            return tuple(carry)

        sums = lax.fori_loop(0, groups, step, (zero,) * 4)
    line = lax.broadcasted_iota(jnp.int32, (8, block), 0)
    tile = zero
    for i, s in enumerate(sums):
        tile = jnp.where(line == i, jnp.sum(s, axis=0, keepdims=True), tile)
    core = place_ref[2]
    for ref, k in ((keep_ref, core), (send_ref, 1 - core)):
        ref[:block, :] = total_ref[pl.ds(pl.multiple_of(k * block, block), block), :]
        ref[block:, :block] = tile
        ref[block:, block:] = tile


def filter_kernel(row_step, count, held_ref, z_ref, params_ref, dxhat_ref, got_ref, out_ref, pad):
    groups, pixels = held_ref.shape[:2]
    rows, block = pad.shape[1], pad.shape[3]
    width = pixels // rows
    share = block // 2
    fill_padded(held_ref, pad)
    got = jnp.sum(got_ref[...], axis=0)
    lines = (got.shape[0] - 8) // 2
    seconds = got[2 * lines :] / count
    params = params_ref[...]
    zero = jnp.zeros((8, block), f32)
    grads = []
    for k in range(2):

        def step(g, carry, k=k):
            carry = list(carry)
            xhat = (z_ref[k, g].astype(f32) - params[2 * k : 2 * k + 1]) * params[2 * k + 1 : 2 * k + 2]
            inner = dxhat_ref[k, g] - seconds[2 * k : 2 * k + 1] - xhat * seconds[2 * k + 1 : 2 * k + 2]
            dz = (params[2 * k + 1 : 2 * k + 2] * inner).astype(bf16).astype(f32).reshape(rows, width, block)
            for a in range(3):
                for b in range(3):
                    moved = tap(pad, g, k, a, b, row_step, width, groups)
                    carry[3 * a + b] = carry[3 * a + b] + fold(dz * moved)
            return tuple(carry)

        grads.append([jnp.sum(s, axis=0, keepdims=True) for s in lax.fori_loop(0, groups, step, (zero,) * 9)])
    line = lax.broadcasted_iota(jnp.int32, (16, block), 0)
    tiles = []
    for k in range(2):
        tile = jnp.zeros((16, block), f32)
        for t in range(9):
            tile = jnp.where(line == t, grads[k][t], tile)
        tiles.append(tile)
    low = lax.broadcasted_iota(jnp.int32, (16, block), 1) < share
    halves = (
        jnp.where(low, tiles[0], pltpu.roll(tiles[1], share, 1)),
        jnp.where(low, pltpu.roll(tiles[0], share, 1), tiles[1]),
    )
    for i in range(out_ref.shape[0]):
        out_ref[i, :lines, :] = got[i % 2 * lines : (i % 2 + 1) * lines]
        out_ref[i, lines:, :] = halves[i % 2]


def mix_kernel(whole_ref, maps_ref, out_ref):
    groups, pixels, both = whole_ref.shape
    block = both // 2
    outs = out_ref.shape[1]
    total = jnp.zeros((pixels, outs), f32)
    for g in range(groups):
        for k in range(2):
            total = total + jnp.dot(
                whole_ref[g, :, k * block : (k + 1) * block],
                maps_ref[g * block : (g + 1) * block, k * outs : (k + 1) * outs],
                preferred_element_type=f32,
            )
    out_ref[...] = total.astype(bf16)


def last_kernel(got_ref, pw_ref, dw_ref):
    peers, total, block = got_ref.shape
    share, wide = pw_ref.shape
    lines = total - 16
    lanes = wide // 2 // block
    for i in range(peers):
        k, lane, row = place_of(i)
        left = (k * lanes + lane) * block
        pw_ref[row * lines : (row + 1) * lines, left : left + block] = got_ref[i, :lines, :]
    dw = jnp.sum(got_ref[:, lines:, :], axis=0)
    dw_ref[:, 0, :] = dw[:9, :share]
    dw_ref[:, 1, :] = pltpu.roll(dw, share, 1)[:9, :share]


def body(features, depthwise, pointwise, bn_gain, cotangent):
    _, row_count, width, channels = features.shape
    outs = cotangent.shape[3]
    groups = lax.axis_size(GROUP)
    peers = lax.axis_size(ROWS)
    samples = lax.axis_size(DP)
    cores = lax.axis_size("core")
    block = channels // groups
    share = block // cores
    pixels = row_count * width
    row_step = row_count * cores
    count = float(samples * groups * cores * pixels)
    mine = lax.axis_index(GROUP)
    lead = FAR_DILATION // row_step
    pad = pltpu.VMEM((groups + 2 * lead, row_count, width + 2 * FAR_DILATION, block), f32)
    lines = share * 2 * outs // peers // block

    (sent,) = call(pack_kernel, "pack", [((groups, pixels, block), bf16, None)], features.reshape(pixels, channels), slow=(0,))
    held = exchange(sent, GROUP)
    cot = cotangent.reshape(1, pixels, outs)
    pairs = [jnp.concatenate([cot, lax.ppermute(cot, "xh", [(0, 1), (1, 0)])], axis=0)]
    pair = pairs[0]
    near = jnp.concatenate([shifted(pair, 1), pair, shifted(pair, -1)], axis=0)
    held, near = lax.optimization_barrier((held, near))
    pairs = [near, shifted(near, 3), shifted(near[:4], -3)]
    taps = lax.dynamic_slice_in_dim(depthwise, mine * block, block, 2).astype(f32).reshape(18, block)
    gain = lax.dynamic_slice_in_dim(bn_gain, mine * block, block, 1)
    maps = lax.dynamic_slice_in_dim(pointwise, mine * block, block, 0)
    maps = maps.reshape(block, 2, outs).transpose(2, 1, 0).reshape(outs, 2 * block)

    z, sums = call(
        functools.partial(forward_kernel, row_step),
        "forward",
        [((2, groups, pixels, block), bf16), ((peers, 8, block), f32, None)],
        held,
        taps,
        scratch=[pad],
    )
    sums = exchange(sums, ROWS)
    sums, *pairs = lax.optimization_barrier((sums, *pairs))
    used, params = call(
        functools.partial(norm_kernel, count),
        "norm",
        [((groups, pixels, 2 * block), bf16, None), ((8, block), f32)],
        z,
        sums,
        gain,
    )
    whole = exchange(used, GROUP)
    dxhat, keep, sent = call(
        back_kernel,
        "back",
        [((2, groups, pixels, block), f32, None)] + [((block + 8, outs), f32)] * 2,
        jnp.stack([lax.axis_index("y"), lax.axis_index("xh"), lax.axis_index("core")]).astype(jnp.int32),
        z,
        params,
        gain,
        *pairs,
        maps,
        slow=range(4, 4 + len(pairs)),
        scratch=[pltpu.VMEM((2 * block, outs), f32), pltpu.VMEM((groups, pixels, outs), bf16)],
        smem=(0,),
    )
    keep = keep + lax.ppermute(sent, "core", [(0, 1), (1, 0)])
    side = lax.axis_index("xl")
    sent = lax.dynamic_slice_in_dim(keep, (1 - side) * block, block, 1)
    keep = lax.dynamic_slice_in_dim(keep, side * block, block, 1)
    keep = keep + lax.ppermute(sent, "xl", [(0, 1), (1, 0)])
    layers = lax.axis_size("z")
    sent = keep[:block].reshape(cores, layers, lines, block).transpose(1, 0, 2, 3).reshape(layers, cores * lines, block)
    sent = jnp.concatenate([sent, jnp.broadcast_to(keep[block:], (layers, 8, block))], axis=1)
    whole, sent = lax.optimization_barrier((whole, sent))
    got = exchange(sent, "z")
    (sent,) = call(
        functools.partial(filter_kernel, row_step, count),
        "filter",
        [((peers, lines + 16, block), f32, None)],
        held,
        z,
        params,
        dxhat,
        got,
        slow=(3,),
        scratch=[pad],
    )
    got = exchange(sent, ROWS)
    (block_out,) = call(mix_kernel, "mix", [((pixels, outs), bf16, None)], whole, pointwise, slow=(1,))
    grad_pw, grad_dw = call(
        last_kernel, "last", [((share, 2 * outs), f32, None), ((9, 2, share), f32, None)], got
    )
    return block_out.reshape(1, row_count, width, outs), grad_pw, grad_dw.transpose(1, 0, 2)


def solution(mesh):
    fine = Mesh(mesh.devices.reshape(8, 2, 8, 2, 2), ("z", "xl", "y", "xh", "core"))
    space = ("y", "xh", "core")
    in_specs = (P(DP, space, None, None), P(), P(), P(), P(DP, space, None, None))
    out_specs = (P(DP, space, None, None), P(space, None), P(None, None, space))
    return jax.shard_map(body, mesh=fine, in_specs=in_specs, out_specs=out_specs, check_vma=False)
```

```python
import functools

import jax
import jax.numpy as jnp
from jax import lax
from jax.experimental import pallas as pl
from jax.experimental.pallas import tpu as pltpu
from jax.sharding import Mesh, PartitionSpec as P

NEAR_DILATION = 12
FAR_DILATION = 24
DILATIONS = (NEAR_DILATION, FAR_DILATION)
eps_norm = 1e-05

GROUP = ("y", "xh")
ORDER = ((-1,), (0,), (1,), (-3, -2), (2, 3), (-4,))
DP = ("z", "xl")
ROWS = ("z", "xl", "core")
f32 = jnp.float32
bf16 = jnp.bfloat16


def exchange(value, axes):
    return lax.all_to_all(value, axes, 0, 0, tiled=True)


def shifted(value, steps):
    count = lax.axis_size("y")
    return lax.ppermute(value, "y", [(i, (i + steps) % count) for i in range(count)])


def call(kernel, outs, *args, scratch=(), smem=(), slow=()):
    vmem = pl.BlockSpec(memory_space=pltpu.VMEM)
    specs = [pl.BlockSpec(memory_space=pltpu.SMEM) if i in smem else vmem for i in range(len(args))]
    args = [
        pltpu.with_memory_space_constraint(a, pltpu.HBM) if i in slow else a for i, a in enumerate(args)
    ]
    return pl.pallas_call(
        kernel,
        out_shape=[pltpu.HBM(*o[:2]) if len(o) == 3 else jax.ShapeDtypeStruct(*o) for o in outs],
        in_specs=specs,
        out_specs=[vmem] * len(outs),
        scratch_shapes=list(scratch),
        compiler_params=pltpu.CompilerParams(vmem_limit_bytes=24 << 20),
    )(*args)


def pack_kernel(feat_ref, out_ref):
    groups, _, block = out_ref.shape
    for g in range(groups):
        out_ref[g] = feat_ref[:, g * block : (g + 1) * block]


def fill_padded(held_ref, pad):
    groups = held_ref.shape[0]
    total, rows, wide, block = pad.shape
    lead = (total - groups) // 2
    width = held_ref.shape[1] // rows
    edge = (wide - width) // 2
    for i in range(lead):
        pad[i] = jnp.zeros((rows, wide, block), f32)
        pad[lead + groups + i] = jnp.zeros((rows, wide, block), f32)

    def step(g, carry):
        value = held_ref[g].astype(f32).reshape(rows, width, block)
        pad[lead + g, :, :edge, :] = jnp.zeros((rows, edge, block), f32)
        pad[lead + g, :, edge + width :, :] = jnp.zeros((rows, edge, block), f32)
        pad[lead + g, :, edge : edge + width, :] = value
        return carry

    lax.fori_loop(0, groups, step, 0)


def tap(pad, g, k, a, b, row_step, width, groups):
    lead = (pad.shape[0] - groups) // 2
    edge = (pad.shape[2] - width) // 2
    row = g + lead + (a - 1) * DILATIONS[k] // row_step
    col = edge + (b - 1) * DILATIONS[k]
    return pad[row, :, col : col + width, :]


def fold(value):
    lanes = value.shape[-1]
    return jnp.sum(value.reshape(-1, 8, lanes), axis=0)


def forward_kernel(row_step, held_ref, taps_ref, z_ref, sums_ref, pad):
    groups, pixels = held_ref.shape[:2]
    rows, block = pad.shape[1], pad.shape[3]
    width = pixels // rows
    fill_padded(held_ref, pad)

    def step(g, carry):
        carry = list(carry)
        for k in range(2):
            total = jnp.zeros((rows, width, block), f32)
            for a in range(3):
                for b in range(3):
                    t = 9 * k + 3 * a + b
                    total = total + taps_ref[t : t + 1, :][None] * tap(pad, g, k, a, b, row_step, width, groups)
            value = total.reshape(pixels, block).astype(bf16)
            z_ref[k, g] = value
            value = value.astype(f32)
            carry[2 * k] = carry[2 * k] + fold(value)
            carry[2 * k + 1] = carry[2 * k + 1] + fold(value * value)
        return tuple(carry)

    zero = jnp.zeros((8, block), f32)
    sums = lax.fori_loop(0, groups, step, (zero,) * 4)
    sums = [jnp.sum(s, axis=0, keepdims=True) for s in sums]
    line = lax.broadcasted_iota(jnp.int32, (8, block), 0)
    tile = zero
    for i, s in enumerate(sums):
        tile = jnp.where(line == i, s, tile)
    for i in range(sums_ref.shape[0]):
        sums_ref[i] = tile


def norm_kernel(count, z_ref, sums_ref, gain_ref, used_ref, params_ref):
    groups, block = z_ref.shape[1], z_ref.shape[3]
    sums = jnp.sum(sums_ref[...], axis=0)
    line = lax.broadcasted_iota(jnp.int32, (8, block), 0)
    tile = jnp.zeros((8, block), f32)
    stats = []
    for k in range(2):
        average = sums[2 * k : 2 * k + 1] / count
        variance = sums[2 * k + 1 : 2 * k + 2] / count - average * average
        inv = lax.rsqrt(variance + eps_norm)
        tile = jnp.where(line == 2 * k, average, tile)
        tile = jnp.where(line == 2 * k + 1, inv, tile)
        stats.append((average, inv))
    params_ref[...] = tile

    def step(g, carry):
        for k in range(2):
            average, inv = stats[k]
            xhat = (z_ref[k, g].astype(f32) - average) * inv
            scaled = gain_ref[k : k + 1, :] * xhat
            used_ref[g, :, k * block : (k + 1) * block] = jnp.maximum(scaled, 0.0).astype(bf16)
        return carry

    lax.fori_loop(0, groups, step, 0)


def place_of(i):
    return i % 2, i // 2 % 2, i // 4


def back_kernel(place_ref, z_ref, params_ref, gain_ref, *refs):
    *pair_refs, maps_ref, dxhat_ref, keep_ref, send_ref, total_ref, cots_ref = refs
    _, groups, _, block = z_ref.shape
    params = params_ref[...]
    gain = gain_ref[...]
    rows, half = groups // 2, place_ref[1]
    zero = jnp.zeros((8, block), f32)
    total_ref[...] = jnp.zeros_like(total_ref)
    for aparts, ref in zip(ORDER, pair_refs, strict=True):
        for i, apart in enumerate(aparts):
            row = (place_ref[0] + apart + rows) % rows
            for slot in range(2):
                cots_ref[2 * row + (half ^ slot)] = ref[2 * i + slot]

    def step(g, carry):
        carry = list(carry)
        cot = cots_ref[g]
        back = jnp.dot(cot, maps_ref[...], preferred_element_type=f32)
        used = []
        for k in range(2):
            xhat = (z_ref[k, g].astype(f32) - params[2 * k : 2 * k + 1]) * params[2 * k + 1 : 2 * k + 2]
            scaled = gain[k : k + 1] * xhat
            used.append(jnp.maximum(scaled, 0.0).astype(bf16))
            dxhat = jnp.where(scaled > 0, back[:, k * block : (k + 1) * block], 0.0) * gain[k : k + 1]
            dxhat_ref[k, g] = dxhat
            carry[2 * k] = carry[2 * k] + fold(dxhat)
            carry[2 * k + 1] = carry[2 * k + 1] + fold(dxhat * xhat)
        for k in range(2):
            total_ref[k * block : (k + 1) * block, :] += lax.dot_general(
                used[k], cot, (((0,), (0,)), ((), ())), preferred_element_type=f32
            )
        return tuple(carry)

    sums = lax.fori_loop(0, groups, step, (zero,) * 4)
    line = lax.broadcasted_iota(jnp.int32, (8, block), 0)
    tile = zero
    for i, s in enumerate(sums):
        tile = jnp.where(line == i, jnp.sum(s, axis=0, keepdims=True), tile)
    core = place_ref[2]
    for ref, k in ((keep_ref, core), (send_ref, 1 - core)):
        ref[:block, :] = total_ref[pl.ds(pl.multiple_of(k * block, block), block), :]
        ref[block:, :block] = tile
        ref[block:, block:] = tile


def filter_kernel(row_step, count, held_ref, z_ref, params_ref, dxhat_ref, got_ref, out_ref, pad):
    groups, pixels = held_ref.shape[:2]
    rows, block = pad.shape[1], pad.shape[3]
    width = pixels // rows
    share = block // 2
    fill_padded(held_ref, pad)
    got = jnp.sum(got_ref[...], axis=0)
    lines = (got.shape[0] - 8) // 2
    seconds = got[2 * lines :] / count
    params = params_ref[...]
    zero = jnp.zeros((8, block), f32)
    grads = []
    for k in range(2):

        def step(g, carry, k=k):
            carry = list(carry)
            xhat = (z_ref[k, g].astype(f32) - params[2 * k : 2 * k + 1]) * params[2 * k + 1 : 2 * k + 2]
            inner = dxhat_ref[k, g] - seconds[2 * k : 2 * k + 1] - xhat * seconds[2 * k + 1 : 2 * k + 2]
            dz = (params[2 * k + 1 : 2 * k + 2] * inner).astype(bf16).astype(f32).reshape(rows, width, block)
            for a in range(3):
                for b in range(3):
                    moved = tap(pad, g, k, a, b, row_step, width, groups)
                    carry[3 * a + b] = carry[3 * a + b] + fold(dz * moved)
            return tuple(carry)

        grads.append([jnp.sum(s, axis=0, keepdims=True) for s in lax.fori_loop(0, groups, step, (zero,) * 9)])
    line = lax.broadcasted_iota(jnp.int32, (16, block), 0)
    tiles = []
    for k in range(2):
        tile = jnp.zeros((16, block), f32)
        for t in range(9):
            tile = jnp.where(line == t, grads[k][t], tile)
        tiles.append(tile)
    low = lax.broadcasted_iota(jnp.int32, (16, block), 1) < share
    halves = (
        jnp.where(low, tiles[0], pltpu.roll(tiles[1], share, 1)),
        jnp.where(low, pltpu.roll(tiles[0], share, 1), tiles[1]),
    )
    for i in range(out_ref.shape[0]):
        out_ref[i, :lines, :] = got[i % 2 * lines : (i % 2 + 1) * lines]
        out_ref[i, lines:, :] = halves[i % 2]


def mix_kernel(whole_ref, maps_ref, out_ref):
    groups, pixels, both = whole_ref.shape
    block = both // 2
    outs = out_ref.shape[1]
    total = jnp.zeros((pixels, outs), f32)
    for g in range(groups):
        for k in range(2):
            total = total + jnp.dot(
                whole_ref[g, :, k * block : (k + 1) * block],
                maps_ref[g * block : (g + 1) * block, k * outs : (k + 1) * outs],
                preferred_element_type=f32,
            )
    out_ref[...] = total.astype(bf16)


def last_kernel(got_ref, pw_ref, dw_ref):
    peers, total, block = got_ref.shape
    share, wide = pw_ref.shape
    lines = total - 16
    lanes = wide // 2 // block
    for i in range(peers):
        k, lane, row = place_of(i)
        left = (k * lanes + lane) * block
        pw_ref[row * lines : (row + 1) * lines, left : left + block] = got_ref[i, :lines, :]
    dw = jnp.sum(got_ref[:, lines:, :], axis=0)
    dw_ref[:, 0, :] = dw[:9, :share]
    dw_ref[:, 1, :] = pltpu.roll(dw, share, 1)[:9, :share]


def body(features, depthwise, pointwise, bn_gain, cotangent):
    _, row_count, width, channels = features.shape
    outs = cotangent.shape[3]
    groups = lax.axis_size(GROUP)
    peers = lax.axis_size(ROWS)
    samples = lax.axis_size(DP)
    cores = lax.axis_size("core")
    block = channels // groups
    share = block // cores
    pixels = row_count * width
    row_step = row_count * cores
    count = float(samples * groups * cores * pixels)
    mine = lax.axis_index(GROUP)
    lead = FAR_DILATION // row_step
    pad = pltpu.VMEM((groups + 2 * lead, row_count, width + 2 * FAR_DILATION, block), f32)
    lines = share * 2 * outs // peers // block

    (sent,) = call(pack_kernel, [((groups, pixels, block), bf16, None)], features.reshape(pixels, channels), slow=(0,))
    held = exchange(sent, GROUP)
    cot = cotangent.reshape(1, pixels, outs)
    pairs = [jnp.concatenate([cot, lax.ppermute(cot, "xh", [(0, 1), (1, 0)])], axis=0)]
    pair = pairs[0]
    above, below = shifted(pair, 1), shifted(pair, -1)
    left, right = jnp.concatenate([above, pair], axis=0), jnp.concatenate([pair, below], axis=0)
    taps = lax.dynamic_slice_in_dim(depthwise, mine * block, block, 2).astype(f32).reshape(18, block)
    held, left, right, taps = lax.optimization_barrier((held, left, right, taps))
    gain = lax.dynamic_slice_in_dim(bn_gain, mine * block, block, 1)
    maps = lax.dynamic_slice_in_dim(pointwise, mine * block, block, 0)
    maps = maps.reshape(block, 2, outs).transpose(2, 1, 0).reshape(outs, 2 * block)

    z, sums = call(
        functools.partial(forward_kernel, row_step),
        [((2, groups, pixels, block), bf16), ((peers, 8, block), f32, None)],
        held,
        taps,
        scratch=[pad],
    )
    sums, left, right = lax.optimization_barrier((sums, left, right))
    sums = exchange(sums, ROWS)
    left = shifted(left, 2)
    right = shifted(right, -2)
    pairs = [above, pair, below, left, right, shifted(left[:2], 1)]
    used, params = call(
        functools.partial(norm_kernel, count),
        [((groups, pixels, 2 * block), bf16, None), ((8, block), f32)],
        z,
        sums,
        gain,
    )
    whole = exchange(used, GROUP)
    dxhat, keep, sent = call(
        back_kernel,
        [((2, groups, pixels, block), f32, None)] + [((block + 8, outs), f32)] * 2,
        jnp.stack([lax.axis_index("y"), lax.axis_index("xh"), lax.axis_index("core")]).astype(jnp.int32),
        z,
        params,
        gain,
        *pairs,
        maps,
        slow=range(4, 4 + len(pairs)),
        scratch=[pltpu.VMEM((2 * block, outs), f32), pltpu.VMEM((groups, pixels, outs), bf16)],
        smem=(0,),
    )
    keep = keep + lax.ppermute(sent, "core", [(0, 1), (1, 0)])
    side = lax.axis_index("xl")
    sent = lax.dynamic_slice_in_dim(keep, (1 - side) * block, block, 1)
    keep = lax.dynamic_slice_in_dim(keep, side * block, block, 1)
    keep = keep + lax.ppermute(sent, "xl", [(0, 1), (1, 0)])
    layers = lax.axis_size("z")
    sent = keep[:block].reshape(cores, layers, lines, block).transpose(1, 0, 2, 3).reshape(layers, cores * lines, block)
    sent = jnp.concatenate([sent, jnp.broadcast_to(keep[block:], (layers, 8, block))], axis=1)
    whole, sent = lax.optimization_barrier((whole, sent))
    got = exchange(sent, "z")
    (sent,) = call(
        functools.partial(filter_kernel, row_step, count),
        [((peers, lines + 16, block), f32, None)],
        held,
        z,
        params,
        dxhat,
        got,
        slow=(3,),
        scratch=[pad],
    )
    got = exchange(sent, ROWS)
    (block_out,) = call(mix_kernel, [((pixels, outs), bf16, None)], whole, pointwise, slow=(1,))
    grad_pw, grad_dw = call(last_kernel, [((share, 2 * outs), f32, None), ((9, 2, share), f32, None)], got)
    return block_out.reshape(1, row_count, width, outs), grad_pw, grad_dw.transpose(1, 0, 2)


def solution(mesh):
    fine = Mesh(mesh.devices.reshape(8, 2, 8, 2, 2), ("z", "xl", "y", "xh", "core"))
    space = ("y", "xh", "core")
    in_specs = (P(DP, space, None, None), P(), P(), P(), P(DP, space, None, None))
    out_specs = (P(DP, space, None, None), P(space, None), P(None, None, space))
    return jax.shard_map(body, mesh=fine, in_specs=in_specs, out_specs=out_specs, check_vma=False)
```

```python
import functools

import jax
import jax.numpy as jnp
from jax import lax
from jax.experimental import pallas as pl
from jax.experimental.pallas import tpu as pltpu
from jax.sharding import Mesh, PartitionSpec as P

NEAR_DILATION = 12
FAR_DILATION = 24
DILATIONS = (NEAR_DILATION, FAR_DILATION)
eps_norm = 1e-05

GROUP = ("y", "xh")
ORDER = (-3, -2, -1, 0, 1, 2, 3, -4)
DP = ("z", "xl")
ROWS = ("z", "xl", "core")
f32 = jnp.float32
bf16 = jnp.bfloat16


def exchange(value, axes):
    return lax.all_to_all(value, axes, 0, 0, tiled=True)


def shifted(value, steps):
    count = lax.axis_size("y")
    return lax.ppermute(value, "y", [(i, (i + steps) % count) for i in range(count)])


def call(kernel, outs, *args, scratch=(), smem=(), slow=()):
    vmem = pl.BlockSpec(memory_space=pltpu.VMEM)
    specs = [pl.BlockSpec(memory_space=pltpu.SMEM) if i in smem else vmem for i in range(len(args))]
    args = [
        pltpu.with_memory_space_constraint(a, pltpu.HBM) if i in slow else a for i, a in enumerate(args)
    ]
    return pl.pallas_call(
        kernel,
        out_shape=[pltpu.HBM(*o[:2]) if len(o) == 3 else jax.ShapeDtypeStruct(*o) for o in outs],
        in_specs=specs,
        out_specs=[vmem] * len(outs),
        scratch_shapes=list(scratch),
        compiler_params=pltpu.CompilerParams(vmem_limit_bytes=24 << 20),
    )(*args)


def pack_kernel(feat_ref, out_ref):
    groups, _, block = out_ref.shape
    for g in range(groups):
        out_ref[g] = feat_ref[:, g * block : (g + 1) * block]


def fill_padded(held_ref, pad):
    groups = held_ref.shape[0]
    total, rows, wide, block = pad.shape
    lead = (total - groups) // 2
    width = held_ref.shape[1] // rows
    edge = (wide - width) // 2
    for i in range(lead):
        pad[i] = jnp.zeros((rows, wide, block), f32)
        pad[lead + groups + i] = jnp.zeros((rows, wide, block), f32)

    def step(g, carry):
        value = held_ref[g].astype(f32).reshape(rows, width, block)
        pad[lead + g, :, :edge, :] = jnp.zeros((rows, edge, block), f32)
        pad[lead + g, :, edge + width :, :] = jnp.zeros((rows, edge, block), f32)
        pad[lead + g, :, edge : edge + width, :] = value
        return carry

    lax.fori_loop(0, groups, step, 0)


def tap(pad, g, k, a, b, row_step, width, groups):
    lead = (pad.shape[0] - groups) // 2
    edge = (pad.shape[2] - width) // 2
    row = g + lead + (a - 1) * DILATIONS[k] // row_step
    col = edge + (b - 1) * DILATIONS[k]
    return pad[row, :, col : col + width, :]


def fold(value):
    lanes = value.shape[-1]
    return jnp.sum(value.reshape(-1, 8, lanes), axis=0)


def forward_kernel(row_step, held_ref, taps_ref, z_ref, sums_ref, pad):
    groups, pixels = held_ref.shape[:2]
    rows, block = pad.shape[1], pad.shape[3]
    width = pixels // rows
    fill_padded(held_ref, pad)

    def step(g, carry):
        carry = list(carry)
        for k in range(2):
            total = jnp.zeros((rows, width, block), f32)
            for a in range(3):
                for b in range(3):
                    t = 9 * k + 3 * a + b
                    total = total + taps_ref[t : t + 1, :][None] * tap(pad, g, k, a, b, row_step, width, groups)
            value = total.reshape(pixels, block).astype(bf16)
            z_ref[k, g] = value
            value = value.astype(f32)
            carry[2 * k] = carry[2 * k] + fold(value)
            carry[2 * k + 1] = carry[2 * k + 1] + fold(value * value)
        return tuple(carry)

    zero = jnp.zeros((8, block), f32)
    sums = lax.fori_loop(0, groups, step, (zero,) * 4)
    sums = [jnp.sum(s, axis=0, keepdims=True) for s in sums]
    line = lax.broadcasted_iota(jnp.int32, (8, block), 0)
    tile = zero
    for i, s in enumerate(sums):
        tile = jnp.where(line == i, s, tile)
    for i in range(sums_ref.shape[0]):
        sums_ref[i] = tile


def norm_kernel(count, z_ref, sums_ref, gain_ref, used_ref, params_ref):
    groups, block = z_ref.shape[1], z_ref.shape[3]
    sums = jnp.sum(sums_ref[...], axis=0)
    line = lax.broadcasted_iota(jnp.int32, (8, block), 0)
    tile = jnp.zeros((8, block), f32)
    stats = []
    for k in range(2):
        average = sums[2 * k : 2 * k + 1] / count
        variance = sums[2 * k + 1 : 2 * k + 2] / count - average * average
        inv = lax.rsqrt(variance + eps_norm)
        tile = jnp.where(line == 2 * k, average, tile)
        tile = jnp.where(line == 2 * k + 1, inv, tile)
        stats.append((average, inv))
    params_ref[...] = tile

    def step(g, carry):
        for k in range(2):
            average, inv = stats[k]
            xhat = (z_ref[k, g].astype(f32) - average) * inv
            scaled = gain_ref[k : k + 1, :] * xhat
            used_ref[g, :, k * block : (k + 1) * block] = jnp.maximum(scaled, 0.0).astype(bf16)
        return carry

    lax.fori_loop(0, groups, step, 0)


def place_of(i):
    return i % 2, i // 2 % 2, i // 4


def back_kernel(place_ref, z_ref, params_ref, gain_ref, *refs):
    *pair_refs, maps_ref, dxhat_ref, keep_ref, send_ref, total_ref, cots_ref = refs
    _, groups, _, block = z_ref.shape
    params = params_ref[...]
    gain = gain_ref[...]
    rows, half = groups // 2, place_ref[1]
    zero = jnp.zeros((8, block), f32)
    total_ref[...] = jnp.zeros_like(total_ref)
    for slot, ref in enumerate(pair_refs):
        for i, apart in enumerate(ORDER):
            row = (place_ref[0] + apart + rows) % rows
            cots_ref[2 * row + (half ^ slot)] = ref[i]

    def step(g, carry):
        carry = list(carry)
        cot = cots_ref[g]
        back = jnp.dot(cot, maps_ref[...], preferred_element_type=f32)
        used = []
        for k in range(2):
            xhat = (z_ref[k, g].astype(f32) - params[2 * k : 2 * k + 1]) * params[2 * k + 1 : 2 * k + 2]
            scaled = gain[k : k + 1] * xhat
            used.append(jnp.maximum(scaled, 0.0).astype(bf16))
            dxhat = jnp.where(scaled > 0, back[:, k * block : (k + 1) * block], 0.0) * gain[k : k + 1]
            dxhat_ref[k, g] = dxhat
            carry[2 * k] = carry[2 * k] + fold(dxhat)
            carry[2 * k + 1] = carry[2 * k + 1] + fold(dxhat * xhat)
        for k in range(2):
            total_ref[k * block : (k + 1) * block, :] += lax.dot_general(
                used[k], cot, (((0,), (0,)), ((), ())), preferred_element_type=f32
            )
        return tuple(carry)

    sums = lax.fori_loop(0, groups, step, (zero,) * 4)
    line = lax.broadcasted_iota(jnp.int32, (8, block), 0)
    tile = zero
    for i, s in enumerate(sums):
        tile = jnp.where(line == i, jnp.sum(s, axis=0, keepdims=True), tile)
    core = place_ref[2]
    for ref, k in ((keep_ref, core), (send_ref, 1 - core)):
        ref[:block, :] = total_ref[pl.ds(pl.multiple_of(k * block, block), block), :]
        ref[block:, :block] = tile
        ref[block:, block:] = tile


def filter_kernel(row_step, count, held_ref, z_ref, params_ref, dxhat_ref, got_ref, out_ref, pad):
    groups, pixels = held_ref.shape[:2]
    rows, block = pad.shape[1], pad.shape[3]
    width = pixels // rows
    share = block // 2
    fill_padded(held_ref, pad)
    got = jnp.sum(got_ref[...], axis=0)
    lines = (got.shape[0] - 8) // 2
    seconds = got[2 * lines :] / count
    params = params_ref[...]
    zero = jnp.zeros((8, block), f32)
    grads = []
    for k in range(2):

        def step(g, carry, k=k):
            carry = list(carry)
            xhat = (z_ref[k, g].astype(f32) - params[2 * k : 2 * k + 1]) * params[2 * k + 1 : 2 * k + 2]
            inner = dxhat_ref[k, g] - seconds[2 * k : 2 * k + 1] - xhat * seconds[2 * k + 1 : 2 * k + 2]
            dz = (params[2 * k + 1 : 2 * k + 2] * inner).astype(bf16).astype(f32).reshape(rows, width, block)
            for a in range(3):
                for b in range(3):
                    moved = tap(pad, g, k, a, b, row_step, width, groups)
                    carry[3 * a + b] = carry[3 * a + b] + fold(dz * moved)
            return tuple(carry)

        grads.append([jnp.sum(s, axis=0, keepdims=True) for s in lax.fori_loop(0, groups, step, (zero,) * 9)])
    line = lax.broadcasted_iota(jnp.int32, (16, block), 0)
    tiles = []
    for k in range(2):
        tile = jnp.zeros((16, block), f32)
        for t in range(9):
            tile = jnp.where(line == t, grads[k][t], tile)
        tiles.append(tile)
    low = lax.broadcasted_iota(jnp.int32, (16, block), 1) < share
    halves = (
        jnp.where(low, tiles[0], pltpu.roll(tiles[1], share, 1)),
        jnp.where(low, pltpu.roll(tiles[0], share, 1), tiles[1]),
    )
    for i in range(out_ref.shape[0]):
        out_ref[i, :lines, :] = got[i % 2 * lines : (i % 2 + 1) * lines]
        out_ref[i, lines:, :] = halves[i % 2]


def mix_kernel(whole_ref, maps_ref, out_ref):
    groups, pixels, both = whole_ref.shape
    block = both // 2
    outs = out_ref.shape[1]
    total = jnp.zeros((pixels, outs), f32)
    for g in range(groups):
        for k in range(2):
            total = total + jnp.dot(
                whole_ref[g, :, k * block : (k + 1) * block],
                maps_ref[g * block : (g + 1) * block, k * outs : (k + 1) * outs],
                preferred_element_type=f32,
            )
    out_ref[...] = total.astype(bf16)


def last_kernel(got_ref, pw_ref, dw_ref):
    peers, total, block = got_ref.shape
    share, wide = pw_ref.shape
    lines = total - 16
    lanes = wide // 2 // block
    for i in range(peers):
        k, lane, row = place_of(i)
        left = (k * lanes + lane) * block
        pw_ref[row * lines : (row + 1) * lines, left : left + block] = got_ref[i, :lines, :]
    dw = jnp.sum(got_ref[:, lines:, :], axis=0)
    dw_ref[:, 0, :] = dw[:9, :share]
    dw_ref[:, 1, :] = pltpu.roll(dw, share, 1)[:9, :share]


def body(features, depthwise, pointwise, bn_gain, cotangent):
    _, row_count, width, channels = features.shape
    outs = cotangent.shape[3]
    groups = lax.axis_size(GROUP)
    peers = lax.axis_size(ROWS)
    samples = lax.axis_size(DP)
    cores = lax.axis_size("core")
    block = channels // groups
    share = block // cores
    pixels = row_count * width
    row_step = row_count * cores
    count = float(samples * groups * cores * pixels)
    mine = lax.axis_index(GROUP)
    lead = FAR_DILATION // row_step
    pad = pltpu.VMEM((groups + 2 * lead, row_count, width + 2 * FAR_DILATION, block), f32)
    lines = share * 2 * outs // peers // block

    (sent,) = call(pack_kernel, [((groups, pixels, block), bf16, None)], features.reshape(pixels, channels), slow=(0,))
    held = exchange(sent, GROUP)
    cot = cotangent.reshape(1, pixels, outs)
    above = shifted(cot, 1)
    below = shifted(cot, -1)
    left = shifted(jnp.concatenate([above, cot], axis=0), 2)
    right = shifted(jnp.concatenate([cot, below], axis=0), -2)
    far = shifted(cot, 4)
    taps = lax.dynamic_slice_in_dim(depthwise, mine * block, block, 2).astype(f32).reshape(18, block)
    held, taps = lax.optimization_barrier((held, taps))
    gain = lax.dynamic_slice_in_dim(bn_gain, mine * block, block, 1)
    maps = lax.dynamic_slice_in_dim(pointwise, mine * block, block, 0)
    maps = maps.reshape(block, 2, outs).transpose(2, 1, 0).reshape(outs, 2 * block)

    z, sums = call(
        functools.partial(forward_kernel, row_step),
        [((2, groups, pixels, block), bf16), ((peers, 8, block), f32, None)],
        held,
        taps,
        scratch=[pad],
    )
    sums = exchange(sums, ROWS)
    column = jnp.concatenate([left, above, cot, below, right, far], axis=0)
    other = lax.ppermute(column, "xh", [(0, 1), (1, 0)])
    pairs = [column, other]
    used, params = call(
        functools.partial(norm_kernel, count),
        [((groups, pixels, 2 * block), bf16, None), ((8, block), f32)],
        z,
        sums,
        gain,
    )
    whole = exchange(used, GROUP)
    dxhat, keep, sent = call(
        back_kernel,
        [((2, groups, pixels, block), f32, None)] + [((block + 8, outs), f32)] * 2,
        jnp.stack([lax.axis_index("y"), lax.axis_index("xh"), lax.axis_index("core")]).astype(jnp.int32),
        z,
        params,
        gain,
        *pairs,
        maps,
        slow=range(4, 4 + len(pairs)),
        scratch=[pltpu.VMEM((2 * block, outs), f32), pltpu.VMEM((groups, pixels, outs), bf16)],
        smem=(0,),
    )
    keep = keep + lax.ppermute(sent, "core", [(0, 1), (1, 0)])
    side = lax.axis_index("xl")
    sent = lax.dynamic_slice_in_dim(keep, (1 - side) * block, block, 1)
    keep = lax.dynamic_slice_in_dim(keep, side * block, block, 1)
    keep = keep + lax.ppermute(sent, "xl", [(0, 1), (1, 0)])
    layers = lax.axis_size("z")
    sent = keep[:block].reshape(cores, layers, lines, block).transpose(1, 0, 2, 3).reshape(layers, cores * lines, block)
    sent = jnp.concatenate([sent, jnp.broadcast_to(keep[block:], (layers, 8, block))], axis=1)
    whole, sent = lax.optimization_barrier((whole, sent))
    got = exchange(sent, "z")
    (sent,) = call(
        functools.partial(filter_kernel, row_step, count),
        [((peers, lines + 16, block), f32, None)],
        held,
        z,
        params,
        dxhat,
        got,
        slow=(3,),
        scratch=[pad],
    )
    got = exchange(sent, ROWS)
    (block_out,) = call(mix_kernel, [((pixels, outs), bf16, None)], whole, pointwise, slow=(1,))
    grad_pw, grad_dw = call(last_kernel, [((share, 2 * outs), f32, None), ((9, 2, share), f32, None)], got)
    return block_out.reshape(1, row_count, width, outs), grad_pw, grad_dw.transpose(1, 0, 2)


def solution(mesh):
    fine = Mesh(mesh.devices.reshape(8, 2, 8, 2, 2), ("z", "xl", "y", "xh", "core"))
    space = ("y", "xh", "core")
    in_specs = (P(DP, space, None, None), P(), P(), P(), P(DP, space, None, None))
    out_specs = (P(DP, space, None, None), P(space, None), P(None, None, space))
    return jax.shard_map(body, mesh=fine, in_specs=in_specs, out_specs=out_specs, check_vma=False)
```

```python
import functools

import jax
import jax.numpy as jnp
from jax import lax
from jax.experimental import pallas as pl
from jax.experimental.pallas import tpu as pltpu
from jax.sharding import Mesh, PartitionSpec as P

NEAR_DILATION = 12
FAR_DILATION = 24
DILATIONS = (NEAR_DILATION, FAR_DILATION)
eps_norm = 1e-05

GROUP = ("y", "xh")
ORDER = (-4, -3, -2, -1, 0, 1, 2, 3)
DP = ("z", "xl")
ROWS = ("z", "xl", "core")
f32 = jnp.float32
bf16 = jnp.bfloat16


def exchange(value, axes):
    return lax.all_to_all(value, axes, 0, 0, tiled=True)


def shifted(value, steps):
    count = lax.axis_size("y")
    return lax.ppermute(value, "y", [(i, (i + steps) % count) for i in range(count)])


def call(kernel, outs, *args, scratch=(), smem=(), slow=()):
    vmem = pl.BlockSpec(memory_space=pltpu.VMEM)
    specs = [pl.BlockSpec(memory_space=pltpu.SMEM) if i in smem else vmem for i in range(len(args))]
    args = [
        pltpu.with_memory_space_constraint(a, pltpu.HBM) if i in slow else a for i, a in enumerate(args)
    ]
    return pl.pallas_call(
        kernel,
        out_shape=[pltpu.HBM(*o[:2]) if len(o) == 3 else jax.ShapeDtypeStruct(*o) for o in outs],
        in_specs=specs,
        out_specs=[vmem] * len(outs),
        scratch_shapes=list(scratch),
        compiler_params=pltpu.CompilerParams(vmem_limit_bytes=24 << 20),
    )(*args)


def pack_kernel(feat_ref, out_ref):
    groups, _, block = out_ref.shape
    for g in range(groups):
        out_ref[g] = feat_ref[:, g * block : (g + 1) * block]


def column_kernel(left_ref, near_ref, right_ref, out_ref):
    out_ref[:3] = left_ref[...]
    out_ref[3:6] = near_ref[...]
    out_ref[6:] = right_ref[...]


def fill_padded(held_ref, pad):
    groups = held_ref.shape[0]
    total, rows, wide, block = pad.shape
    lead = (total - groups) // 2
    width = held_ref.shape[1] // rows
    edge = (wide - width) // 2
    for i in range(lead):
        pad[i] = jnp.zeros((rows, wide, block), f32)
        pad[lead + groups + i] = jnp.zeros((rows, wide, block), f32)

    def step(g, carry):
        value = held_ref[g].astype(f32).reshape(rows, width, block)
        pad[lead + g, :, :edge, :] = jnp.zeros((rows, edge, block), f32)
        pad[lead + g, :, edge + width :, :] = jnp.zeros((rows, edge, block), f32)
        pad[lead + g, :, edge : edge + width, :] = value
        return carry

    lax.fori_loop(0, groups, step, 0)


def tap(pad, g, k, a, b, row_step, width, groups):
    lead = (pad.shape[0] - groups) // 2
    edge = (pad.shape[2] - width) // 2
    row = g + lead + (a - 1) * DILATIONS[k] // row_step
    col = edge + (b - 1) * DILATIONS[k]
    return pad[row, :, col : col + width, :]


def fold(value):
    lanes = value.shape[-1]
    return jnp.sum(value.reshape(-1, 8, lanes), axis=0)


def forward_kernel(row_step, held_ref, taps_ref, z_ref, sums_ref, pad):
    groups, pixels = held_ref.shape[:2]
    rows, block = pad.shape[1], pad.shape[3]
    width = pixels // rows
    fill_padded(held_ref, pad)

    def step(g, carry):
        carry = list(carry)
        for k in range(2):
            total = jnp.zeros((rows, width, block), f32)
            for a in range(3):
                for b in range(3):
                    t = 9 * k + 3 * a + b
                    total = total + taps_ref[t : t + 1, :][None] * tap(pad, g, k, a, b, row_step, width, groups)
            value = total.reshape(pixels, block).astype(bf16)
            z_ref[k, g] = value
            value = value.astype(f32)
            carry[2 * k] = carry[2 * k] + fold(value)
            carry[2 * k + 1] = carry[2 * k + 1] + fold(value * value)
        return tuple(carry)

    zero = jnp.zeros((8, block), f32)
    sums = lax.fori_loop(0, groups, step, (zero,) * 4)
    sums = [jnp.sum(s, axis=0, keepdims=True) for s in sums]
    line = lax.broadcasted_iota(jnp.int32, (8, block), 0)
    tile = zero
    for i, s in enumerate(sums):
        tile = jnp.where(line == i, s, tile)
    for i in range(sums_ref.shape[0]):
        sums_ref[i] = tile[:4]


def norm_kernel(count, z_ref, sums_ref, gain_ref, used_ref, params_ref):
    groups, block = z_ref.shape[1], z_ref.shape[3]
    sums = jnp.sum(sums_ref[...], axis=0)
    line = lax.broadcasted_iota(jnp.int32, (8, block), 0)
    tile = jnp.zeros((8, block), f32)
    stats = []
    for k in range(2):
        average = sums[2 * k : 2 * k + 1] / count
        variance = sums[2 * k + 1 : 2 * k + 2] / count - average * average
        inv = lax.rsqrt(variance + eps_norm)
        tile = jnp.where(line == 2 * k, average, tile)
        tile = jnp.where(line == 2 * k + 1, inv, tile)
        stats.append((average, inv))
    params_ref[...] = tile

    def step(g, carry):
        for k in range(2):
            average, inv = stats[k]
            xhat = (z_ref[k, g].astype(f32) - average) * inv
            scaled = gain_ref[k : k + 1, :] * xhat
            used_ref[g, :, k * block : (k + 1) * block] = jnp.maximum(scaled, 0.0).astype(bf16)
        return carry

    lax.fori_loop(0, groups, step, 0)


def place_of(i):
    return i % 2, i // 2 % 2, i // 4


def back_kernel(place_ref, z_ref, params_ref, gain_ref, *refs):
    *pair_refs, maps_ref, dxhat_ref, keep_ref, send_ref, total_ref, cots_ref = refs
    _, groups, _, block = z_ref.shape
    params = params_ref[...]
    gain = gain_ref[...]
    rows, half = groups // 2, place_ref[1]
    zero = jnp.zeros((8, block), f32)
    total_ref[...] = jnp.zeros_like(total_ref)
    for slot, ref in enumerate(pair_refs):
        for i, apart in enumerate(ORDER):
            row = (place_ref[0] + apart + rows) % rows
            cots_ref[2 * row + (half ^ slot)] = ref[i]

    def step(g, carry):
        carry = list(carry)
        cot = cots_ref[g]
        back = jnp.dot(cot, maps_ref[...], preferred_element_type=f32)
        used = []
        for k in range(2):
            xhat = (z_ref[k, g].astype(f32) - params[2 * k : 2 * k + 1]) * params[2 * k + 1 : 2 * k + 2]
            scaled = gain[k : k + 1] * xhat
            used.append(jnp.maximum(scaled, 0.0).astype(bf16))
            dxhat = jnp.where(scaled > 0, back[:, k * block : (k + 1) * block], 0.0) * gain[k : k + 1]
            dxhat_ref[k, g] = dxhat
            carry[2 * k] = carry[2 * k] + fold(dxhat)
            carry[2 * k + 1] = carry[2 * k + 1] + fold(dxhat * xhat)
        for k in range(2):
            total_ref[k * block : (k + 1) * block, :] += lax.dot_general(
                used[k], cot, (((0,), (0,)), ((), ())), preferred_element_type=f32
            )
        return tuple(carry)

    sums = lax.fori_loop(0, groups, step, (zero,) * 4)
    line = lax.broadcasted_iota(jnp.int32, (8, block), 0)
    tile = zero
    for i, s in enumerate(sums):
        tile = jnp.where(line == i, jnp.sum(s, axis=0, keepdims=True), tile)
    core = place_ref[2]
    for ref, k in ((keep_ref, core), (send_ref, 1 - core)):
        ref[:block, :] = total_ref[pl.ds(pl.multiple_of(k * block, block), block), :]
        ref[block:, :block] = tile
        ref[block:, block:] = tile


def filter_kernel(row_step, count, held_ref, z_ref, params_ref, dxhat_ref, got_ref, out_ref, pad):
    groups, pixels = held_ref.shape[:2]
    rows, block = pad.shape[1], pad.shape[3]
    width = pixels // rows
    share = block // 2
    fill_padded(held_ref, pad)
    got = jnp.sum(got_ref[...], axis=0)
    lines = (got.shape[0] - 8) // 2
    seconds = got[2 * lines :] / count
    params = params_ref[...]
    zero = jnp.zeros((8, block), f32)
    grads = []
    for k in range(2):

        def step(g, carry, k=k):
            carry = list(carry)
            xhat = (z_ref[k, g].astype(f32) - params[2 * k : 2 * k + 1]) * params[2 * k + 1 : 2 * k + 2]
            inner = dxhat_ref[k, g] - seconds[2 * k : 2 * k + 1] - xhat * seconds[2 * k + 1 : 2 * k + 2]
            dz = (params[2 * k + 1 : 2 * k + 2] * inner).astype(bf16).astype(f32).reshape(rows, width, block)
            for a in range(3):
                for b in range(3):
                    moved = tap(pad, g, k, a, b, row_step, width, groups)
                    carry[3 * a + b] = carry[3 * a + b] + fold(dz * moved)
            return tuple(carry)

        grads.append([jnp.sum(s, axis=0, keepdims=True) for s in lax.fori_loop(0, groups, step, (zero,) * 9)])
    line = lax.broadcasted_iota(jnp.int32, (16, block), 0)
    tiles = []
    for k in range(2):
        tile = jnp.zeros((16, block), f32)
        for t in range(9):
            tile = jnp.where(line == t, grads[k][t], tile)
        tiles.append(tile)
    low = lax.broadcasted_iota(jnp.int32, (16, block), 1) < share
    halves = (
        jnp.where(low, tiles[0], pltpu.roll(tiles[1], share, 1)),
        jnp.where(low, pltpu.roll(tiles[0], share, 1), tiles[1]),
    )
    for i in range(out_ref.shape[0]):
        out_ref[i, :lines, :] = got[i % 2 * lines : (i % 2 + 1) * lines]
        out_ref[i, lines:, :] = halves[i % 2]


def mix_kernel(whole_ref, maps_ref, out_ref):
    groups, pixels, both = whole_ref.shape
    block = both // 2
    outs = out_ref.shape[1]
    total = jnp.zeros((pixels, outs), f32)
    for g in range(groups):
        for k in range(2):
            total = total + jnp.dot(
                whole_ref[g, :, k * block : (k + 1) * block],
                maps_ref[g * block : (g + 1) * block, k * outs : (k + 1) * outs],
                preferred_element_type=f32,
            )
    out_ref[...] = total.astype(bf16)


def last_kernel(got_ref, pw_ref, dw_ref):
    peers, total, block = got_ref.shape
    share, wide = pw_ref.shape
    lines = total - 16
    lanes = wide // 2 // block
    for i in range(peers):
        k, lane, row = place_of(i)
        left = (k * lanes + lane) * block
        pw_ref[row * lines : (row + 1) * lines, left : left + block] = got_ref[i, :lines, :]
    dw = jnp.sum(got_ref[:, lines:, :], axis=0)
    dw_ref[:, 0, :] = dw[:9, :share]
    dw_ref[:, 1, :] = pltpu.roll(dw, share, 1)[:9, :share]


def body(features, depthwise, pointwise, bn_gain, cotangent):
    _, row_count, width, channels = features.shape
    outs = cotangent.shape[3]
    groups = lax.axis_size(GROUP)
    peers = lax.axis_size(ROWS)
    samples = lax.axis_size(DP)
    cores = lax.axis_size("core")
    block = channels // groups
    share = block // cores
    pixels = row_count * width
    row_step = row_count * cores
    count = float(samples * groups * cores * pixels)
    mine = lax.axis_index(GROUP)
    lead = FAR_DILATION // row_step
    pad = pltpu.VMEM((groups + 2 * lead, row_count, width + 2 * FAR_DILATION, block), f32)
    lines = share * 2 * outs // peers // block

    (sent,) = call(pack_kernel, [((groups, pixels, block), bf16, None)], features.reshape(pixels, channels), slow=(0,))
    held = exchange(sent, GROUP)
    cot = cotangent.reshape(1, pixels, outs)
    above = shifted(cot, 1)
    below = shifted(cot, -1)
    near = jnp.concatenate([above, cot, below], axis=0)
    left = shifted(near, 3)
    right = shifted(near[:2], -3)
    taps = lax.dynamic_slice_in_dim(depthwise, mine * block, block, 2).astype(f32).reshape(18, block)
    held, taps = lax.optimization_barrier((held, taps))
    gain = lax.dynamic_slice_in_dim(bn_gain, mine * block, block, 1)
    maps = lax.dynamic_slice_in_dim(pointwise, mine * block, block, 0)
    maps = maps.reshape(block, 2, outs).transpose(2, 1, 0).reshape(outs, 2 * block)

    z, sums = call(
        functools.partial(forward_kernel, row_step),
        [((2, groups, pixels, block), bf16), ((peers, 4, block), f32, None)],
        held,
        taps,
        scratch=[pad],
    )
    sums = exchange(sums, ROWS)
    (column,) = call(column_kernel, [((8, pixels, outs), bf16, None)], left, near, right)
    other = lax.ppermute(column, "xh", [(0, 1), (1, 0)])
    pairs = [column, other]
    used, params = call(
        functools.partial(norm_kernel, count),
        [((groups, pixels, 2 * block), bf16, None), ((8, block), f32)],
        z,
        sums,
        gain,
    )
    whole = exchange(used, GROUP)
    dxhat, keep, sent = call(
        back_kernel,
        [((2, groups, pixels, block), f32, None)] + [((block + 8, outs), f32)] * 2,
        jnp.stack([lax.axis_index("y"), lax.axis_index("xh"), lax.axis_index("core")]).astype(jnp.int32),
        z,
        params,
        gain,
        *pairs,
        maps,
        slow=range(4, 4 + len(pairs)),
        scratch=[pltpu.VMEM((2 * block, outs), f32), pltpu.VMEM((groups, pixels, outs), bf16)],
        smem=(0,),
    )
    keep = keep + lax.ppermute(sent, "core", [(0, 1), (1, 0)])
    side = lax.axis_index("xl")
    sent = lax.dynamic_slice_in_dim(keep, (1 - side) * block, block, 1)
    keep = lax.dynamic_slice_in_dim(keep, side * block, block, 1)
    keep = keep + lax.ppermute(sent, "xl", [(0, 1), (1, 0)])
    layers = lax.axis_size("z")
    sent = keep[:block].reshape(cores, layers, lines, block).transpose(1, 0, 2, 3).reshape(layers, cores * lines, block)
    sent = jnp.concatenate([sent, jnp.broadcast_to(keep[block:], (layers, 8, block))], axis=1)
    whole, sent = lax.optimization_barrier((whole, sent))
    got = exchange(sent, "z")
    (sent,) = call(
        functools.partial(filter_kernel, row_step, count),
        [((peers, lines + 16, block), f32, None)],
        held,
        z,
        params,
        dxhat,
        got,
        slow=(3,),
        scratch=[pad],
    )
    got = exchange(sent, ROWS)
    (block_out,) = call(mix_kernel, [((pixels, outs), bf16, None)], whole, pointwise, slow=(1,))
    grad_pw, grad_dw = call(last_kernel, [((share, 2 * outs), f32, None), ((9, 2, share), f32, None)], got)
    return block_out.reshape(1, row_count, width, outs), grad_pw, grad_dw.transpose(1, 0, 2)


def solution(mesh):
    fine = Mesh(mesh.devices.reshape(8, 2, 8, 2, 2), ("z", "xl", "y", "xh", "core"))
    space = ("y", "xh", "core")
    in_specs = (P(DP, space, None, None), P(), P(), P(), P(DP, space, None, None))
    out_specs = (P(DP, space, None, None), P(space, None), P(None, None, space))
    return jax.shard_map(body, mesh=fine, in_specs=in_specs, out_specs=out_specs, check_vma=False)
```

```python
import functools

import jax
import jax.numpy as jnp
from jax import lax
from jax.experimental import pallas as pl
from jax.experimental.pallas import tpu as pltpu
from jax.sharding import Mesh, PartitionSpec as P

NEAR_DILATION = 12
FAR_DILATION = 24
DILATIONS = (NEAR_DILATION, FAR_DILATION)
eps_norm = 1e-05

GROUP = ("y", "xh")
ORDER = (-4, -3, -2, -1, 0, 1, 2, 3)
DP = ("z", "xl")
ROWS = ("z", "xl", "core")
f32 = jnp.float32
bf16 = jnp.bfloat16


def exchange(value, axes):
    return lax.all_to_all(value, axes, 0, 0, tiled=True)


def shifted(value, steps):
    count = lax.axis_size("y")
    return lax.ppermute(value, "y", [(i, (i + steps) % count) for i in range(count)])


def call(kernel, outs, *args, scratch=(), smem=(), slow=()):
    vmem = pl.BlockSpec(memory_space=pltpu.VMEM)
    specs = [pl.BlockSpec(memory_space=pltpu.SMEM) if i in smem else vmem for i in range(len(args))]
    args = [
        pltpu.with_memory_space_constraint(a, pltpu.HBM) if i in slow else a for i, a in enumerate(args)
    ]
    return pl.pallas_call(
        kernel,
        out_shape=[pltpu.HBM(*o[:2]) if len(o) == 3 else jax.ShapeDtypeStruct(*o) for o in outs],
        in_specs=specs,
        out_specs=[vmem] * len(outs),
        scratch_shapes=list(scratch),
        compiler_params=pltpu.CompilerParams(vmem_limit_bytes=24 << 20),
    )(*args)


def pack_kernel(feat_ref, out_ref):
    groups, _, block = out_ref.shape
    for g in range(groups):
        out_ref[g] = feat_ref[:, g * block : (g + 1) * block]


def column_kernel(left_ref, near_ref, right_ref, out_ref):
    out_ref[:3] = left_ref[...]
    out_ref[3:6] = near_ref[...]
    out_ref[6:] = right_ref[...]


def fill_padded(held_ref, pad):
    groups = held_ref.shape[0]
    total, rows, wide, block = pad.shape
    lead = (total - groups) // 2
    width = held_ref.shape[1] // rows
    edge = (wide - width) // 2
    for i in range(lead):
        pad[i] = jnp.zeros((rows, wide, block), f32)
        pad[lead + groups + i] = jnp.zeros((rows, wide, block), f32)

    def step(g, carry):
        value = held_ref[g].astype(f32).reshape(rows, width, block)
        pad[lead + g, :, :edge, :] = jnp.zeros((rows, edge, block), f32)
        pad[lead + g, :, edge + width :, :] = jnp.zeros((rows, edge, block), f32)
        pad[lead + g, :, edge : edge + width, :] = value
        return carry

    lax.fori_loop(0, groups, step, 0)


def tap(pad, g, k, a, b, row_step, width, groups):
    lead = (pad.shape[0] - groups) // 2
    edge = (pad.shape[2] - width) // 2
    row = g + lead + (a - 1) * DILATIONS[k] // row_step
    col = edge + (b - 1) * DILATIONS[k]
    return pad[row, :, col : col + width, :]


def fold(value):
    lanes = value.shape[-1]
    return jnp.sum(value.reshape(-1, 8, lanes), axis=0)


def forward_kernel(row_step, held_ref, taps_ref, z_ref, sums_ref, pad):
    groups, pixels = held_ref.shape[:2]
    rows, block = pad.shape[1], pad.shape[3]
    width = pixels // rows
    fill_padded(held_ref, pad)

    def step(g, carry):
        carry = list(carry)
        for k in range(2):
            total = jnp.zeros((rows, width, block), f32)
            for a in range(3):
                for b in range(3):
                    t = 9 * k + 3 * a + b
                    total = total + taps_ref[t : t + 1, :][None] * tap(pad, g, k, a, b, row_step, width, groups)
            value = total.reshape(pixels, block).astype(bf16)
            z_ref[k, g] = value
            value = value.astype(f32)
            carry[2 * k] = carry[2 * k] + fold(value)
            carry[2 * k + 1] = carry[2 * k + 1] + fold(value * value)
        return tuple(carry)

    zero = jnp.zeros((8, block), f32)
    sums = lax.fori_loop(0, groups, step, (zero,) * 4)
    sums = [jnp.sum(s, axis=0, keepdims=True) for s in sums]
    line = lax.broadcasted_iota(jnp.int32, (8, block), 0)
    tile = zero
    for i, s in enumerate(sums):
        tile = jnp.where(line == i, s, tile)
    for i in range(sums_ref.shape[0]):
        sums_ref[i] = tile[:4]


def norm_kernel(count, z_ref, sums_ref, gain_ref, used_ref, params_ref):
    groups, block = z_ref.shape[1], z_ref.shape[3]
    sums = jnp.sum(sums_ref[...], axis=0)
    line = lax.broadcasted_iota(jnp.int32, (8, block), 0)
    tile = jnp.zeros((8, block), f32)
    stats = []
    for k in range(2):
        average = sums[2 * k : 2 * k + 1] / count
        variance = sums[2 * k + 1 : 2 * k + 2] / count - average * average
        inv = lax.rsqrt(variance + eps_norm)
        tile = jnp.where(line == 2 * k, average, tile)
        tile = jnp.where(line == 2 * k + 1, inv, tile)
        stats.append((average, inv))
    params_ref[...] = tile

    def step(g, carry):
        for k in range(2):
            average, inv = stats[k]
            xhat = (z_ref[k, g].astype(f32) - average) * inv
            scaled = gain_ref[k : k + 1, :] * xhat
            used_ref[g, :, k * block : (k + 1) * block] = jnp.maximum(scaled, 0.0).astype(bf16)
        return carry

    lax.fori_loop(0, groups, step, 0)


def place_of(i):
    return i % 2, i // 2 % 2, i // 4


def back_kernel(place_ref, z_ref, params_ref, gain_ref, *refs):
    *pair_refs, maps_ref, dxhat_ref, keep_ref, send_ref, total_ref, cots_ref = refs
    _, groups, _, block = z_ref.shape
    outs = total_ref.shape[1]
    params = params_ref[...]
    gain = gain_ref[...]
    rows, half = groups // 2, place_ref[1]
    zero = jnp.zeros((8, block), f32)
    total_ref[...] = jnp.zeros_like(total_ref)
    for slot, ref in enumerate(pair_refs):
        for i, apart in enumerate(ORDER):
            row = (place_ref[0] + apart + rows) % rows
            cots_ref[2 * row + (half ^ slot)] = ref[i]

    def step(g, carry):
        carry = list(carry)
        cot = cots_ref[g]
        used = []
        for k in range(2):
            xhat = (z_ref[k, g].astype(f32) - params[2 * k : 2 * k + 1]) * params[2 * k + 1 : 2 * k + 2]
            scaled = gain[k : k + 1] * xhat
            used.append(jnp.maximum(scaled, 0.0).astype(bf16))
            back = lax.dot_general(
                cot, maps_ref[:, k * outs : (k + 1) * outs], (((1,), (1,)), ((), ())), preferred_element_type=f32
            )
            dxhat = jnp.where(scaled > 0, back, 0.0) * gain[k : k + 1]
            dxhat_ref[k, g] = dxhat
            carry[2 * k] = carry[2 * k] + fold(dxhat)
            carry[2 * k + 1] = carry[2 * k + 1] + fold(dxhat * xhat)
        for k in range(2):
            total_ref[k * block : (k + 1) * block, :] += lax.dot_general(
                used[k], cot, (((0,), (0,)), ((), ())), preferred_element_type=f32
            )
        return tuple(carry)

    sums = lax.fori_loop(0, groups, step, (zero,) * 4)
    line = lax.broadcasted_iota(jnp.int32, (8, block), 0)
    tile = zero
    for i, s in enumerate(sums):
        tile = jnp.where(line == i, jnp.sum(s, axis=0, keepdims=True), tile)
    core = place_ref[2]
    for ref, k in ((keep_ref, core), (send_ref, 1 - core)):
        ref[:block, :] = total_ref[pl.ds(pl.multiple_of(k * block, block), block), :]
        ref[block:, :block] = tile
        ref[block:, block:] = tile


def filter_kernel(row_step, count, held_ref, z_ref, params_ref, dxhat_ref, got_ref, out_ref, pad):
    groups, pixels = held_ref.shape[:2]
    rows, block = pad.shape[1], pad.shape[3]
    width = pixels // rows
    share = block // 2
    fill_padded(held_ref, pad)
    got = jnp.sum(got_ref[...], axis=0)
    lines = (got.shape[0] - 8) // 2
    seconds = got[2 * lines :] / count
    params = params_ref[...]
    zero = jnp.zeros((8, block), f32)
    grads = []
    for k in range(2):

        def step(g, carry, k=k):
            carry = list(carry)
            xhat = (z_ref[k, g].astype(f32) - params[2 * k : 2 * k + 1]) * params[2 * k + 1 : 2 * k + 2]
            inner = dxhat_ref[k, g] - seconds[2 * k : 2 * k + 1] - xhat * seconds[2 * k + 1 : 2 * k + 2]
            dz = (params[2 * k + 1 : 2 * k + 2] * inner).astype(bf16).astype(f32).reshape(rows, width, block)
            for a in range(3):
                for b in range(3):
                    moved = tap(pad, g, k, a, b, row_step, width, groups)
                    carry[3 * a + b] = carry[3 * a + b] + fold(dz * moved)
            return tuple(carry)

        grads.append([jnp.sum(s, axis=0, keepdims=True) for s in lax.fori_loop(0, groups, step, (zero,) * 9)])
    line = lax.broadcasted_iota(jnp.int32, (16, block), 0)
    tiles = []
    for k in range(2):
        tile = jnp.zeros((16, block), f32)
        for t in range(9):
            tile = jnp.where(line == t, grads[k][t], tile)
        tiles.append(tile)
    low = lax.broadcasted_iota(jnp.int32, (16, block), 1) < share
    halves = (
        jnp.where(low, tiles[0], pltpu.roll(tiles[1], share, 1)),
        jnp.where(low, pltpu.roll(tiles[0], share, 1), tiles[1]),
    )
    for i in range(out_ref.shape[0]):
        out_ref[i, :lines, :] = got[i % 2 * lines : (i % 2 + 1) * lines]
        out_ref[i, lines:, :] = halves[i % 2]


def mix_kernel(whole_ref, maps_ref, out_ref):
    groups, pixels, both = whole_ref.shape
    block = both // 2
    outs = out_ref.shape[1]
    total = jnp.zeros((pixels, outs), f32)
    for g in range(groups):
        for k in range(2):
            total = total + jnp.dot(
                whole_ref[g, :, k * block : (k + 1) * block],
                maps_ref[g * block : (g + 1) * block, k * outs : (k + 1) * outs],
                preferred_element_type=f32,
            )
    out_ref[...] = total.astype(bf16)


def last_kernel(got_ref, pw_ref, dw_ref):
    peers, total, block = got_ref.shape
    share, wide = pw_ref.shape
    lines = total - 16
    lanes = wide // 2 // block
    for i in range(peers):
        k, lane, row = place_of(i)
        left = (k * lanes + lane) * block
        pw_ref[row * lines : (row + 1) * lines, left : left + block] = got_ref[i, :lines, :]
    dw = jnp.sum(got_ref[:, lines:, :], axis=0)
    dw_ref[:, 0, :] = dw[:9, :share]
    dw_ref[:, 1, :] = pltpu.roll(dw, share, 1)[:9, :share]


def body(features, depthwise, pointwise, bn_gain, cotangent):
    _, row_count, width, channels = features.shape
    outs = cotangent.shape[3]
    groups = lax.axis_size(GROUP)
    peers = lax.axis_size(ROWS)
    samples = lax.axis_size(DP)
    cores = lax.axis_size("core")
    block = channels // groups
    share = block // cores
    pixels = row_count * width
    row_step = row_count * cores
    count = float(samples * groups * cores * pixels)
    mine = lax.axis_index(GROUP)
    lead = FAR_DILATION // row_step
    pad = pltpu.VMEM((groups + 2 * lead, row_count, width + 2 * FAR_DILATION, block), f32)
    lines = share * 2 * outs // peers // block

    (sent,) = call(pack_kernel, [((groups, pixels, block), bf16, None)], features.reshape(pixels, channels), slow=(0,))
    held = exchange(sent, GROUP)
    cot = cotangent.reshape(1, pixels, outs)
    above = shifted(cot, 1)
    below = shifted(cot, -1)
    near = jnp.concatenate([above, cot, below], axis=0)
    left = shifted(near, 3)
    right = shifted(near[:2], -3)
    taps = lax.dynamic_slice_in_dim(depthwise, mine * block, block, 2).astype(f32).reshape(18, block)
    held, taps = lax.optimization_barrier((held, taps))
    gain = lax.dynamic_slice_in_dim(bn_gain, mine * block, block, 1)
    maps = lax.dynamic_slice_in_dim(pointwise, mine * block, block, 0)

    z, sums = call(
        functools.partial(forward_kernel, row_step),
        [((2, groups, pixels, block), bf16), ((peers, 4, block), f32, None)],
        held,
        taps,
        scratch=[pad],
    )
    sums = exchange(sums, ROWS)
    (column,) = call(column_kernel, [((8, pixels, outs), bf16, None)], left, near, right)
    other = lax.ppermute(column, "xh", [(0, 1), (1, 0)])
    pairs = [column, other]
    sums, gain, maps = lax.optimization_barrier((sums, gain, maps))
    used, params = call(
        functools.partial(norm_kernel, count),
        [((groups, pixels, 2 * block), bf16, None), ((8, block), f32)],
        z,
        sums,
        gain,
    )
    whole = exchange(used, GROUP)
    dxhat, keep, sent = call(
        back_kernel,
        [((2, groups, pixels, block), f32, None)] + [((block + 8, outs), f32)] * 2,
        jnp.stack([lax.axis_index("y"), lax.axis_index("xh"), lax.axis_index("core")]).astype(jnp.int32),
        z,
        params,
        gain,
        *pairs,
        maps,
        slow=range(4, 4 + len(pairs)),
        scratch=[pltpu.VMEM((2 * block, outs), f32), pltpu.VMEM((groups, pixels, outs), bf16)],
        smem=(0,),
    )
    keep = keep + lax.ppermute(sent, "core", [(0, 1), (1, 0)])
    side = lax.axis_index("xl")
    sent = lax.dynamic_slice_in_dim(keep, (1 - side) * block, block, 1)
    keep = lax.dynamic_slice_in_dim(keep, side * block, block, 1)
    keep = keep + lax.ppermute(sent, "xl", [(0, 1), (1, 0)])
    layers = lax.axis_size("z")
    sent = keep[:block].reshape(cores, layers, lines, block).transpose(1, 0, 2, 3).reshape(layers, cores * lines, block)
    sent = jnp.concatenate([sent, jnp.broadcast_to(keep[block:], (layers, 8, block))], axis=1)
    whole, sent = lax.optimization_barrier((whole, sent))
    got = exchange(sent, "z")
    (sent,) = call(
        functools.partial(filter_kernel, row_step, count),
        [((peers, lines + 16, block), f32, None)],
        held,
        z,
        params,
        dxhat,
        got,
        slow=(3,),
        scratch=[pad],
    )
    got = exchange(sent, ROWS)
    (block_out,) = call(mix_kernel, [((pixels, outs), bf16, None)], whole, pointwise, slow=(1,))
    grad_pw, grad_dw = call(last_kernel, [((share, 2 * outs), f32, None), ((9, 2, share), f32, None)], got)
    return block_out.reshape(1, row_count, width, outs), grad_pw, grad_dw.transpose(1, 0, 2)


def solution(mesh):
    fine = Mesh(mesh.devices.reshape(8, 2, 8, 2, 2), ("z", "xl", "y", "xh", "core"))
    space = ("y", "xh", "core")
    in_specs = (P(DP, space, None, None), P(), P(), P(), P(DP, space, None, None))
    out_specs = (P(DP, space, None, None), P(space, None), P(None, None, space))
    return jax.shard_map(body, mesh=fine, in_specs=in_specs, out_specs=out_specs, check_vma=False)
```

```python
import functools

import jax
import jax.numpy as jnp
from jax import lax
from jax.experimental import pallas as pl
from jax.experimental.pallas import tpu as pltpu
from jax.sharding import Mesh, PartitionSpec as P

NEAR_DILATION = 12
FAR_DILATION = 24
DILATIONS = (NEAR_DILATION, FAR_DILATION)
eps_norm = 1e-05

GROUP = ("y", "xh")
ORDER = (-4, -3, -2, -1, 0, 1, 2, 3)
DP = ("z", "xl")
ROWS = ("z", "xl", "core")
f32 = jnp.float32
bf16 = jnp.bfloat16


def exchange(value, axes):
    return lax.all_to_all(value, axes, 0, 0, tiled=True)


def shifted(value, steps):
    count = lax.axis_size("y")
    return lax.ppermute(value, "y", [(i, (i + steps) % count) for i in range(count)])


def call(kernel, outs, *args, scratch=(), smem=(), slow=()):
    vmem = pl.BlockSpec(memory_space=pltpu.VMEM)
    specs = [pl.BlockSpec(memory_space=pltpu.SMEM) if i in smem else vmem for i in range(len(args))]
    args = [
        pltpu.with_memory_space_constraint(a, pltpu.HBM) if i in slow else a for i, a in enumerate(args)
    ]
    return pl.pallas_call(
        kernel,
        out_shape=[pltpu.HBM(*o[:2]) if len(o) == 3 else jax.ShapeDtypeStruct(*o) for o in outs],
        in_specs=specs,
        out_specs=[vmem] * len(outs),
        scratch_shapes=list(scratch),
        compiler_params=pltpu.CompilerParams(vmem_limit_bytes=24 << 20),
    )(*args)


def pack_kernel(feat_ref, out_ref):
    groups, _, block = out_ref.shape
    for g in range(groups):
        out_ref[g] = feat_ref[:, g * block : (g + 1) * block]


def column_kernel(left_ref, near_ref, right_ref, out_ref):
    out_ref[:3] = left_ref[...]
    out_ref[3:6] = near_ref[...]
    out_ref[6:] = right_ref[...]


def fill_padded(held_ref, pad):
    groups = held_ref.shape[0]
    total, rows, wide, block = pad.shape
    lead = (total - groups) // 2
    width = held_ref.shape[1] // rows
    edge = (wide - width) // 2
    for i in range(lead):
        pad[i] = jnp.zeros((rows, wide, block), f32)
        pad[lead + groups + i] = jnp.zeros((rows, wide, block), f32)

    def step(g, carry):
        value = held_ref[g].astype(f32).reshape(rows, width, block)
        pad[lead + g, :, :edge, :] = jnp.zeros((rows, edge, block), f32)
        pad[lead + g, :, edge + width :, :] = jnp.zeros((rows, edge, block), f32)
        pad[lead + g, :, edge : edge + width, :] = value
        return carry

    lax.fori_loop(0, groups, step, 0)


def tap(pad, g, k, a, b, row_step, width, groups):
    lead = (pad.shape[0] - groups) // 2
    edge = (pad.shape[2] - width) // 2
    row = g + lead + (a - 1) * DILATIONS[k] // row_step
    col = edge + (b - 1) * DILATIONS[k]
    return pad[row, :, col : col + width, :]


def fold(value):
    lanes = value.shape[-1]
    return jnp.sum(value.reshape(-1, 8, lanes), axis=0)


def forward_kernel(row_step, held_ref, taps_ref, z_ref, sums_ref, pad):
    groups, pixels = held_ref.shape[:2]
    rows, block = pad.shape[1], pad.shape[3]
    width = pixels // rows
    fill_padded(held_ref, pad)

    def step(g, carry):
        carry = list(carry)
        for k in range(2):
            total = jnp.zeros((rows, width, block), f32)
            for a in range(3):
                for b in range(3):
                    t = 9 * k + 3 * a + b
                    total = total + taps_ref[t : t + 1, :][None] * tap(pad, g, k, a, b, row_step, width, groups)
            value = total.reshape(pixels, block).astype(bf16)
            z_ref[k, g] = value
            value = value.astype(f32)
            carry[2 * k] = carry[2 * k] + fold(value)
            carry[2 * k + 1] = carry[2 * k + 1] + fold(value * value)
        return tuple(carry)

    zero = jnp.zeros((8, block), f32)
    sums = lax.fori_loop(0, groups, step, (zero,) * 4)
    sums = [jnp.sum(s, axis=0, keepdims=True) for s in sums]
    line = lax.broadcasted_iota(jnp.int32, (8, block), 0)
    tile = zero
    for i, s in enumerate(sums):
        tile = jnp.where(line == i, s, tile)
    for i in range(sums_ref.shape[0]):
        sums_ref[i] = tile[:4]


def norm_kernel(count, z_ref, sums_ref, gain_ref, used_ref, params_ref):
    groups, block = z_ref.shape[1], z_ref.shape[3]
    sums = jnp.sum(sums_ref[...], axis=0)
    line = lax.broadcasted_iota(jnp.int32, (8, block), 0)
    tile = jnp.zeros((8, block), f32)
    stats = []
    for k in range(2):
        average = sums[2 * k : 2 * k + 1] / count
        variance = sums[2 * k + 1 : 2 * k + 2] / count - average * average
        inv = lax.rsqrt(variance + eps_norm)
        tile = jnp.where(line == 2 * k, average, tile)
        tile = jnp.where(line == 2 * k + 1, inv, tile)
        stats.append((average, inv))
    params_ref[...] = tile

    def step(g, carry):
        for k in range(2):
            average, inv = stats[k]
            xhat = (z_ref[k, g].astype(f32) - average) * inv
            scaled = gain_ref[k : k + 1, :] * xhat
            used_ref[g, :, k * block : (k + 1) * block] = jnp.maximum(scaled, 0.0).astype(bf16)
        return carry

    lax.fori_loop(0, groups, step, 0)


def place_of(i):
    return i % 2, i // 2 % 2, i // 4


def back_kernel(place_ref, z_ref, params_ref, gain_ref, *refs):
    *pair_refs, maps_ref, dxhat_ref, keep_ref, send_ref, total_ref, cots_ref = refs
    _, groups, _, block = z_ref.shape
    outs = total_ref.shape[1]
    params = params_ref[...]
    gain = gain_ref[...]
    rows, half = groups // 2, place_ref[1]
    zero = jnp.zeros((8, block), f32)
    total_ref[...] = jnp.zeros_like(total_ref)
    for slot, ref in enumerate(pair_refs):
        for i, apart in enumerate(ORDER):
            row = (place_ref[0] + apart + rows) % rows
            cots_ref[2 * row + (half ^ slot)] = ref[i]

    def step(g, carry):
        carry = list(carry)
        cot = cots_ref[g]
        used = []
        for k in range(2):
            xhat = (z_ref[k, g].astype(f32) - params[2 * k : 2 * k + 1]) * params[2 * k + 1 : 2 * k + 2]
            scaled = gain[k : k + 1] * xhat
            used.append(jnp.maximum(scaled, 0.0).astype(bf16))
            back = lax.dot_general(
                cot, maps_ref[:, k * outs : (k + 1) * outs], (((1,), (1,)), ((), ())), preferred_element_type=f32
            )
            dxhat = jnp.where(scaled > 0, back, 0.0) * gain[k : k + 1]
            dxhat_ref[k, g] = dxhat
            carry[2 * k] = carry[2 * k] + fold(dxhat)
            carry[2 * k + 1] = carry[2 * k + 1] + fold(dxhat * xhat)
        for k in range(2):
            total_ref[k * block : (k + 1) * block, :] += lax.dot_general(
                used[k], cot, (((0,), (0,)), ((), ())), preferred_element_type=f32
            )
        return tuple(carry)

    sums = lax.fori_loop(0, groups, step, (zero,) * 4)
    line = lax.broadcasted_iota(jnp.int32, (8, block), 0)
    tile = zero
    for i, s in enumerate(sums):
        tile = jnp.where(line == i, jnp.sum(s, axis=0, keepdims=True), tile)
    core = place_ref[2]
    for ref, k in ((keep_ref, core), (send_ref, 1 - core)):
        ref[:block, :] = total_ref[pl.ds(pl.multiple_of(k * block, block), block), :]
        ref[block:, :block] = tile
        ref[block:, block:] = tile


def filter_kernel(row_step, count, held_ref, z_ref, params_ref, dxhat_ref, got_ref, out_ref, pad):
    groups, pixels = held_ref.shape[:2]
    rows, block = pad.shape[1], pad.shape[3]
    width = pixels // rows
    share = block // 2
    fill_padded(held_ref, pad)
    got = jnp.sum(got_ref[...], axis=0)
    lines = (got.shape[0] - 8) // 2
    seconds = got[2 * lines :] / count
    params = params_ref[...]
    zero = jnp.zeros((8, block), f32)
    grads = []
    for k in range(2):

        def step(g, carry, k=k):
            carry = list(carry)
            xhat = (z_ref[k, g].astype(f32) - params[2 * k : 2 * k + 1]) * params[2 * k + 1 : 2 * k + 2]
            inner = dxhat_ref[k, g] - seconds[2 * k : 2 * k + 1] - xhat * seconds[2 * k + 1 : 2 * k + 2]
            dz = (params[2 * k + 1 : 2 * k + 2] * inner).astype(bf16).astype(f32).reshape(rows, width, block)
            for a in range(3):
                for b in range(3):
                    moved = tap(pad, g, k, a, b, row_step, width, groups)
                    carry[3 * a + b] = carry[3 * a + b] + fold(dz * moved)
            return tuple(carry)

        grads.append([jnp.sum(s, axis=0, keepdims=True) for s in lax.fori_loop(0, groups, step, (zero,) * 9)])
    line = lax.broadcasted_iota(jnp.int32, (16, block), 0)
    tiles = []
    for k in range(2):
        tile = jnp.zeros((16, block), f32)
        for t in range(9):
            tile = jnp.where(line == t, grads[k][t], tile)
        tiles.append(tile)
    low = lax.broadcasted_iota(jnp.int32, (16, block), 1) < share
    halves = (
        jnp.where(low, tiles[0], pltpu.roll(tiles[1], share, 1)),
        jnp.where(low, pltpu.roll(tiles[0], share, 1), tiles[1]),
    )
    for i in range(out_ref.shape[0]):
        rows_sent = [got[i % 2 * lines + 4 * j : i % 2 * lines + 4 * (j + 1)] for j in range(lines // 4)]
        rows_sent += [halves[i % 2][4 * j : 4 * (j + 1)] for j in range(3)]
        for j, value in enumerate(rows_sent):
            out_ref[i, j] = value


def mix_kernel(whole_ref, maps_ref, out_ref):
    groups, pixels, both = whole_ref.shape
    block = both // 2
    outs = out_ref.shape[1]
    total = jnp.zeros((pixels, outs), f32)
    for g in range(groups):
        for k in range(2):
            total = total + jnp.dot(
                whole_ref[g, :, k * block : (k + 1) * block],
                maps_ref[g * block : (g + 1) * block, k * outs : (k + 1) * outs],
                preferred_element_type=f32,
            )
    out_ref[...] = total.astype(bf16)


def last_kernel(got_ref, pw_ref, dw_ref):
    peers, tiles, four, block = got_ref.shape
    share, wide = pw_ref.shape
    tiles -= 3
    lines = tiles * four
    lanes = wide // 2 // block
    for i in range(peers):
        k, lane, row = place_of(i)
        left = (k * lanes + lane) * block
        for j in range(tiles):
            top = row * lines + j * four
            pw_ref[top : top + four, left : left + block] = got_ref[i, j]
    dw = jnp.sum(got_ref[:, tiles:], axis=0)
    for t in range(9):
        line = dw[t // four, t % four : t % four + 1]
        dw_ref[t, 0:1, :] = line[:, :share]
        dw_ref[t, 1:2, :] = pltpu.roll(line, share, 1)[:, :share]


def body(features, depthwise, pointwise, bn_gain, cotangent):
    _, row_count, width, channels = features.shape
    outs = cotangent.shape[3]
    groups = lax.axis_size(GROUP)
    peers = lax.axis_size(ROWS)
    samples = lax.axis_size(DP)
    cores = lax.axis_size("core")
    block = channels // groups
    share = block // cores
    pixels = row_count * width
    row_step = row_count * cores
    count = float(samples * groups * cores * pixels)
    mine = lax.axis_index(GROUP)
    lead = FAR_DILATION // row_step
    pad = pltpu.VMEM((groups + 2 * lead, row_count, width + 2 * FAR_DILATION, block), f32)
    lines = share * 2 * outs // peers // block

    (sent,) = call(pack_kernel, [((groups, pixels, block), bf16)], features.reshape(pixels, channels), slow=(0,))
    held = exchange(sent, GROUP)
    cot = cotangent.reshape(1, pixels, outs)
    above = shifted(cot, 1)
    below = shifted(cot, -1)
    near = jnp.concatenate([above, cot, below], axis=0)
    left = shifted(near, 3)
    right = shifted(near[:2], -3)
    taps = lax.dynamic_slice_in_dim(depthwise, mine * block, block, 2).astype(f32).reshape(18, block)
    held, taps = lax.optimization_barrier((held, taps))
    gain = lax.dynamic_slice_in_dim(bn_gain, mine * block, block, 1)
    maps = lax.dynamic_slice_in_dim(pointwise, mine * block, block, 0)

    z, sums = call(
        functools.partial(forward_kernel, row_step),
        [((2, groups, pixels, block), bf16), ((peers, 4, block), f32)],
        held,
        taps,
        scratch=[pad],
    )
    sums = exchange(sums, ROWS)
    (column,) = call(column_kernel, [((8, pixels, outs), bf16, None)], left, near, right)
    other = lax.ppermute(column, "xh", [(0, 1), (1, 0)])
    pairs = [column, other]
    sums, gain, maps = lax.optimization_barrier((sums, gain, maps))
    used, params = call(
        functools.partial(norm_kernel, count), [((groups, pixels, 2 * block), bf16), ((8, block), f32)], z, sums, gain
    )
    whole = exchange(used, GROUP)
    dxhat, keep, sent = call(
        back_kernel,
        [((2, groups, pixels, block), f32, None)] + [((block + 8, outs), f32)] * 2,
        jnp.stack([lax.axis_index("y"), lax.axis_index("xh"), lax.axis_index("core")]).astype(jnp.int32),
        z,
        params,
        gain,
        *pairs,
        maps,
        slow=range(4, 4 + len(pairs)),
        scratch=[pltpu.VMEM((2 * block, outs), f32), pltpu.VMEM((groups, pixels, outs), bf16)],
        smem=(0,),
    )
    keep = keep + lax.ppermute(sent, "core", [(0, 1), (1, 0)])
    side = lax.axis_index("xl")
    sent = lax.dynamic_slice_in_dim(keep, (1 - side) * block, block, 1)
    keep = lax.dynamic_slice_in_dim(keep, side * block, block, 1)
    keep = keep + lax.ppermute(sent, "xl", [(0, 1), (1, 0)])
    layers = lax.axis_size("z")
    sent = keep[:block].reshape(cores, layers, lines, block).transpose(1, 0, 2, 3).reshape(layers, cores * lines, block)
    sent = jnp.concatenate([sent, jnp.broadcast_to(keep[block:], (layers, 8, block))], axis=1)
    whole, sent = lax.optimization_barrier((whole, sent))
    got = exchange(sent, "z")
    (sent,) = call(
        functools.partial(filter_kernel, row_step, count),
        [((peers, lines // 4 + 3, 4, block), f32)],
        held,
        z,
        params,
        dxhat,
        got,
        slow=(3,),
        scratch=[pad],
    )
    got = exchange(sent, ROWS)
    (block_out,) = call(mix_kernel, [((pixels, outs), bf16, None)], whole, pointwise, slow=(1,))
    grad_pw, grad_dw = call(last_kernel, [((share, 2 * outs), f32, None), ((9, 2, share), f32, None)], got)
    return block_out.reshape(1, row_count, width, outs), grad_pw, grad_dw.transpose(1, 0, 2)


def solution(mesh):
    fine = Mesh(mesh.devices.reshape(8, 2, 8, 2, 2), ("z", "xl", "y", "xh", "core"))
    space = ("y", "xh", "core")
    in_specs = (P(DP, space, None, None), P(), P(), P(), P(DP, space, None, None))
    out_specs = (P(DP, space, None, None), P(space, None), P(None, None, space))
    return jax.shard_map(body, mesh=fine, in_specs=in_specs, out_specs=out_specs, check_vma=False)
```

```python
import functools

import jax
import jax.numpy as jnp
from jax import lax
from jax.experimental import pallas as pl
from jax.experimental.pallas import tpu as pltpu
from jax.sharding import Mesh, PartitionSpec as P

NEAR_DILATION = 12
FAR_DILATION = 24
DILATIONS = (NEAR_DILATION, FAR_DILATION)
eps_norm = 1e-05

GROUP = ("y", "xh")
ORDER = (-2, 0, 2, 4)
DP = ("z", "xl")
ROWS = ("z", "xl", "core")
f32 = jnp.float32
bf16 = jnp.bfloat16


def exchange(value, axes):
    return lax.all_to_all(value, axes, 0, 0, tiled=True)


def shifted(value, steps):
    count = lax.axis_size("y")
    return lax.ppermute(value, "y", [(i, (i + steps) % count) for i in range(count)])


def call(kernel, outs, *args, scratch=(), smem=(), slow=()):
    vmem = pl.BlockSpec(memory_space=pltpu.VMEM)
    specs = [pl.BlockSpec(memory_space=pltpu.SMEM) if i in smem else vmem for i in range(len(args))]
    args = [
        pltpu.with_memory_space_constraint(a, pltpu.HBM) if i in slow else a for i, a in enumerate(args)
    ]
    return pl.pallas_call(
        kernel,
        out_shape=[pltpu.HBM(*o[:2]) if len(o) == 3 else jax.ShapeDtypeStruct(*o) for o in outs],
        in_specs=specs,
        out_specs=[vmem] * len(outs),
        scratch_shapes=list(scratch),
        compiler_params=pltpu.CompilerParams(vmem_limit_bytes=24 << 20),
    )(*args)


def pack_kernel(feat_ref, out_ref):
    groups, _, block = out_ref.shape
    for g in range(groups):
        out_ref[g] = feat_ref[:, g * block : (g + 1) * block]


def column_kernel(*refs):
    *pair_refs, out_ref = refs
    for i, ref in enumerate(pair_refs):
        out_ref[2 * i : 2 * i + 2] = ref[...]


def fill_padded(held_ref, pad):
    groups = held_ref.shape[0]
    total, rows, wide, block = pad.shape
    lead = (total - groups) // 2
    width = held_ref.shape[1] // rows
    edge = (wide - width) // 2
    for i in range(lead):
        pad[i] = jnp.zeros((rows, wide, block), f32)
        pad[lead + groups + i] = jnp.zeros((rows, wide, block), f32)

    def step(g, carry):
        value = held_ref[g].astype(f32).reshape(rows, width, block)
        pad[lead + g, :, :edge, :] = jnp.zeros((rows, edge, block), f32)
        pad[lead + g, :, edge + width :, :] = jnp.zeros((rows, edge, block), f32)
        pad[lead + g, :, edge : edge + width, :] = value
        return carry

    lax.fori_loop(0, groups, step, 0)


def tap(pad, g, k, a, b, row_step, width, groups):
    lead = (pad.shape[0] - groups) // 2
    edge = (pad.shape[2] - width) // 2
    row = g + lead + (a - 1) * DILATIONS[k] // row_step
    col = edge + (b - 1) * DILATIONS[k]
    return pad[row, :, col : col + width, :]


def fold(value):
    lanes = value.shape[-1]
    return jnp.sum(value.reshape(-1, 8, lanes), axis=0)


def forward_kernel(row_step, held_ref, taps_ref, z_ref, sums_ref, pad):
    groups, pixels = held_ref.shape[:2]
    rows, block = pad.shape[1], pad.shape[3]
    width = pixels // rows
    fill_padded(held_ref, pad)

    def step(g, carry):
        carry = list(carry)
        for k in range(2):
            total = jnp.zeros((rows, width, block), f32)
            for a in range(3):
                for b in range(3):
                    t = 9 * k + 3 * a + b
                    total = total + taps_ref[t : t + 1, :][None] * tap(pad, g, k, a, b, row_step, width, groups)
            value = total.reshape(pixels, block).astype(bf16)
            z_ref[k, g] = value
            value = value.astype(f32)
            carry[2 * k] = carry[2 * k] + fold(value)
            carry[2 * k + 1] = carry[2 * k + 1] + fold(value * value)
        return tuple(carry)

    zero = jnp.zeros((8, block), f32)
    sums = lax.fori_loop(0, groups, step, (zero,) * 4)
    sums = [jnp.sum(s, axis=0, keepdims=True) for s in sums]
    line = lax.broadcasted_iota(jnp.int32, (8, block), 0)
    tile = zero
    for i, s in enumerate(sums):
        tile = jnp.where(line == i, s, tile)
    for i in range(sums_ref.shape[0]):
        sums_ref[i] = tile[:4]


def norm_kernel(count, z_ref, sums_ref, gain_ref, used_ref, params_ref):
    groups, block = z_ref.shape[1], z_ref.shape[3]
    sums = jnp.sum(sums_ref[...], axis=0)
    line = lax.broadcasted_iota(jnp.int32, (8, block), 0)
    tile = jnp.zeros((8, block), f32)
    stats = []
    for k in range(2):
        average = sums[2 * k : 2 * k + 1] / count
        variance = sums[2 * k + 1 : 2 * k + 2] / count - average * average
        inv = lax.rsqrt(variance + eps_norm)
        tile = jnp.where(line == 2 * k, average, tile)
        tile = jnp.where(line == 2 * k + 1, inv, tile)
        stats.append((average, inv))
    params_ref[...] = tile

    def step(g, carry):
        for k in range(2):
            average, inv = stats[k]
            xhat = (z_ref[k, g].astype(f32) - average) * inv
            scaled = gain_ref[k : k + 1, :] * xhat
            used_ref[g, :, k * block : (k + 1) * block] = jnp.maximum(scaled, 0.0).astype(bf16)
        return carry

    lax.fori_loop(0, groups, step, 0)


def place_of(i):
    return i % 2, i // 2 % 2, i // 4


def back_kernel(place_ref, z_ref, params_ref, gain_ref, *refs):
    *pair_refs, maps_ref, dxhat_ref, keep_ref, send_ref, total_ref, cots_ref = refs
    _, groups, _, block = z_ref.shape
    outs = total_ref.shape[1]
    params = params_ref[...]
    gain = gain_ref[...]
    rows, half = groups // 2, place_ref[1]
    zero = jnp.zeros((8, block), f32)
    total_ref[...] = jnp.zeros_like(total_ref)
    for slot, ref in enumerate(pair_refs):
        for i, apart in enumerate(ORDER):
            row = (place_ref[0] + apart + rows) % rows
            for j in range(2):
                cots_ref[2 * (row ^ j) + (half ^ slot)] = ref[2 * i + j]

    def step(g, carry):
        carry = list(carry)
        cot = cots_ref[g]
        used = []
        for k in range(2):
            xhat = (z_ref[k, g].astype(f32) - params[2 * k : 2 * k + 1]) * params[2 * k + 1 : 2 * k + 2]
            scaled = gain[k : k + 1] * xhat
            used.append(jnp.maximum(scaled, 0.0).astype(bf16))
            back = lax.dot_general(
                cot, maps_ref[:, k * outs : (k + 1) * outs], (((1,), (1,)), ((), ())), preferred_element_type=f32
            )
            dxhat = jnp.where(scaled > 0, back, 0.0) * gain[k : k + 1]
            dxhat_ref[k, g] = dxhat
            carry[2 * k] = carry[2 * k] + fold(dxhat)
            carry[2 * k + 1] = carry[2 * k + 1] + fold(dxhat * xhat)
        for k in range(2):
            total_ref[k * block : (k + 1) * block, :] += lax.dot_general(
                used[k], cot, (((0,), (0,)), ((), ())), preferred_element_type=f32
            )
        return tuple(carry)

    sums = lax.fori_loop(0, groups, step, (zero,) * 4)
    line = lax.broadcasted_iota(jnp.int32, (8, block), 0)
    tile = zero
    for i, s in enumerate(sums):
        tile = jnp.where(line == i, jnp.sum(s, axis=0, keepdims=True), tile)
    core = place_ref[2]
    for ref, k in ((keep_ref, core), (send_ref, 1 - core)):
        ref[:block, :] = total_ref[pl.ds(pl.multiple_of(k * block, block), block), :]
        ref[block:, :block] = tile
        ref[block:, block:] = tile


def filter_kernel(row_step, count, held_ref, z_ref, params_ref, dxhat_ref, got_ref, out_ref, pad):
    groups, pixels = held_ref.shape[:2]
    rows, block = pad.shape[1], pad.shape[3]
    width = pixels // rows
    share = block // 2
    fill_padded(held_ref, pad)
    got = jnp.sum(got_ref[...], axis=0)
    lines = (got.shape[0] - 8) // 2
    seconds = got[2 * lines :] / count
    params = params_ref[...]
    zero = jnp.zeros((8, block), f32)
    grads = []
    for k in range(2):

        def step(g, carry, k=k):
            carry = list(carry)
            xhat = (z_ref[k, g].astype(f32) - params[2 * k : 2 * k + 1]) * params[2 * k + 1 : 2 * k + 2]
            inner = dxhat_ref[k, g] - seconds[2 * k : 2 * k + 1] - xhat * seconds[2 * k + 1 : 2 * k + 2]
            dz = (params[2 * k + 1 : 2 * k + 2] * inner).astype(bf16).astype(f32).reshape(rows, width, block)
            for a in range(3):
                for b in range(3):
                    moved = tap(pad, g, k, a, b, row_step, width, groups)
                    carry[3 * a + b] = carry[3 * a + b] + fold(dz * moved)
            return tuple(carry)

        grads.append([jnp.sum(s, axis=0, keepdims=True) for s in lax.fori_loop(0, groups, step, (zero,) * 9)])
    line = lax.broadcasted_iota(jnp.int32, (16, block), 0)
    tiles = []
    for k in range(2):
        tile = jnp.zeros((16, block), f32)
        for t in range(9):
            tile = jnp.where(line == t, grads[k][t], tile)
        tiles.append(tile)
    low = lax.broadcasted_iota(jnp.int32, (16, block), 1) < share
    halves = (
        jnp.where(low, tiles[0], pltpu.roll(tiles[1], share, 1)),
        jnp.where(low, pltpu.roll(tiles[0], share, 1), tiles[1]),
    )
    for i in range(out_ref.shape[0]):
        rows_sent = [got[i % 2 * lines + 4 * j : i % 2 * lines + 4 * (j + 1)] for j in range(lines // 4)]
        rows_sent += [halves[i % 2][4 * j : 4 * (j + 1)] for j in range(3)]
        for j, value in enumerate(rows_sent):
            out_ref[i, j] = value


def mix_kernel(whole_ref, maps_ref, out_ref):
    groups, pixels, both = whole_ref.shape
    block = both // 2
    outs = out_ref.shape[1]
    total = jnp.zeros((pixels, outs), f32)
    for g in range(groups):
        for k in range(2):
            total = total + jnp.dot(
                whole_ref[g, :, k * block : (k + 1) * block],
                maps_ref[g * block : (g + 1) * block, k * outs : (k + 1) * outs],
                preferred_element_type=f32,
            )
    out_ref[...] = total.astype(bf16)


def last_kernel(got_ref, pw_ref, dw_ref):
    peers, tiles, four, block = got_ref.shape
    share, wide = pw_ref.shape
    tiles -= 3
    lines = tiles * four
    lanes = wide // 2 // block
    for i in range(peers):
        k, lane, row = place_of(i)
        left = (k * lanes + lane) * block
        for j in range(tiles):
            top = row * lines + j * four
            pw_ref[top : top + four, left : left + block] = got_ref[i, j]
    dw = jnp.sum(got_ref[:, tiles:], axis=0)
    for t in range(9):
        line = dw[t // four, t % four : t % four + 1]
        dw_ref[t, 0:1, :] = line[:, :share]
        dw_ref[t, 1:2, :] = pltpu.roll(line, share, 1)[:, :share]


def body(features, depthwise, pointwise, bn_gain, cotangent):
    _, row_count, width, channels = features.shape
    outs = cotangent.shape[3]
    groups = lax.axis_size(GROUP)
    peers = lax.axis_size(ROWS)
    samples = lax.axis_size(DP)
    cores = lax.axis_size("core")
    block = channels // groups
    share = block // cores
    pixels = row_count * width
    row_step = row_count * cores
    count = float(samples * groups * cores * pixels)
    mine = lax.axis_index(GROUP)
    lead = FAR_DILATION // row_step
    pad = pltpu.VMEM((groups + 2 * lead, row_count, width + 2 * FAR_DILATION, block), f32)
    lines = share * 2 * outs // peers // block

    (sent,) = call(pack_kernel, [((groups, pixels, block), bf16)], features.reshape(pixels, channels), slow=(0,))
    held = exchange(sent, GROUP)
    cot = cotangent.reshape(1, pixels, outs)
    count_y = lax.axis_size("y")
    beside = lax.ppermute(cot, "y", [(i, i ^ 1) for i in range(count_y)])
    near = jnp.concatenate([cot, beside], axis=0)
    left = shifted(near, 2)
    right = shifted(near, -2)
    far = shifted(near, 4)
    taps = lax.dynamic_slice_in_dim(depthwise, mine * block, block, 2).astype(f32).reshape(18, block)
    gain = lax.dynamic_slice_in_dim(bn_gain, mine * block, block, 1)
    maps = lax.dynamic_slice_in_dim(pointwise, mine * block, block, 0)

    held, taps, gain, maps = lax.optimization_barrier((held, taps, gain, maps))
    z, sums = call(
        functools.partial(forward_kernel, row_step),
        [((2, groups, pixels, block), bf16), ((peers, 4, block), f32)],
        held,
        taps,
        scratch=[pad],
    )
    sums = exchange(sums, ROWS)
    (column,) = call(column_kernel, [((8, pixels, outs), bf16, None)], left, near, right, far)
    other = lax.ppermute(column, "xh", [(0, 1), (1, 0)])
    pairs = [column, other]
    used, params = call(
        functools.partial(norm_kernel, count), [((groups, pixels, 2 * block), bf16), ((8, block), f32)], z, sums, gain
    )
    whole = exchange(used, GROUP)
    dxhat, keep, sent = call(
        back_kernel,
        [((2, groups, pixels, block), f32, None)] + [((block + 8, outs), f32)] * 2,
        jnp.stack([lax.axis_index("y"), lax.axis_index("xh"), lax.axis_index("core")]).astype(jnp.int32),
        z,
        params,
        gain,
        *pairs,
        maps,
        slow=range(4, 4 + len(pairs)),
        scratch=[pltpu.VMEM((2 * block, outs), f32), pltpu.VMEM((groups, pixels, outs), bf16)],
        smem=(0,),
    )
    keep = keep + lax.ppermute(sent, "core", [(0, 1), (1, 0)])
    side = lax.axis_index("xl")
    sent = lax.dynamic_slice_in_dim(keep, (1 - side) * block, block, 1)
    keep = lax.dynamic_slice_in_dim(keep, side * block, block, 1)
    keep = keep + lax.ppermute(sent, "xl", [(0, 1), (1, 0)])
    layers = lax.axis_size("z")
    sent = keep[:block].reshape(cores, layers, lines, block).transpose(1, 0, 2, 3).reshape(layers, cores * lines, block)
    sent = jnp.concatenate([sent, jnp.broadcast_to(keep[block:], (layers, 8, block))], axis=1)
    whole, sent = lax.optimization_barrier((whole, sent))
    got = exchange(sent, "z")
    (sent,) = call(
        functools.partial(filter_kernel, row_step, count),
        [((peers, lines // 4 + 3, 4, block), f32)],
        held,
        z,
        params,
        dxhat,
        got,
        slow=(3,),
        scratch=[pad],
    )
    got = exchange(sent, ROWS)
    (block_out,) = call(mix_kernel, [((pixels, outs), bf16, None)], whole, pointwise, slow=(1,))
    grad_pw, grad_dw = call(last_kernel, [((share, 2 * outs), f32, None), ((9, 2, share), f32, None)], got)
    return block_out.reshape(1, row_count, width, outs), grad_pw, grad_dw.transpose(1, 0, 2)


def solution(mesh):
    fine = Mesh(mesh.devices.reshape(8, 2, 8, 2, 2), ("z", "xl", "y", "xh", "core"))
    space = ("y", "xh", "core")
    in_specs = (P(DP, space, None, None), P(), P(), P(), P(DP, space, None, None))
    out_specs = (P(DP, space, None, None), P(space, None), P(None, None, space))
    return jax.shard_map(body, mesh=fine, in_specs=in_specs, out_specs=out_specs, check_vma=False)
```
